512 devices in a mesh: rep: 64 (over x, z), tp: 8 (over y, core).
Axes of the slice: x: 4, y: 4, z: 16, core: 2. Of those that a mesh axis runs over, the one named last changes fastest.
Arguments:
- queries: bfloat16 [8192, 4096], P(('rep', 'tp')), may hold values from -120 to 120
- fresh_kv: bfloat16 [8192, 2048], P(('rep', 'tp')), may hold values from -8 to 8
- kv_pool: bfloat16 [8192, 16, 2048], P('rep', None, 'tp'), may hold values from -6 to 6
- residual: bfloat16 [8192, 4096], P('rep', 'tp'), may hold values from -6 to 6
- norm_gain: float32 [4096], P('tp'), may hold values from 0.1 to 1.9
- gate_up: bfloat16 [64, 4096, 2048], P('rep', None, 'tp'), may hold values from -0.09375 to 0.09375
- down_proj: bfloat16 [64, 1024, 4096], P('rep', None, 'tp'), may hold values from -0.0625 to 0.0625
- prior_len: int32 [256], replicated, may hold values from 1 to 512, as said below
- new_len: int32 [256], replicated, may hold values from 16 to 32, as said below
- page_table: int32 [64, 128], P('rep'), may hold values from 0 to 127, each once within a row
- leaving: int32 [64], replicated, may hold values from 0 to 3
- expert_ids: int32 [8192, 2], P('rep'), may hold values from 0 to 7, all different within a row; in each aligned block of 128 rows (0 to 127, 128 to 255, ...) at most 40 rows name the same one
- route_logits: float32 [8192, 2], P('rep'), may hold values from -6 to 6
Outputs:
- output: bfloat16 [8192, 4096], P('rep', 'tp')
The draws below stay inside these ranges and needn't reach their ends.
Inputs may be any that keep to these rules, and one draw needn't show every extreme that they name: `prior_len`: some request has exactly 512 earlier tokens. `new_len`: some request has exactly 32 live new tokens. `page_table`: each group's row names each of its 128 pages once. `expert_ids`: the two experts of a slot differ; among the 128 slots of one group no expert is named more than 40 times, and in some group one is named exactly 40 times.
All inputs are finite; a program needn't handle non-finite values.
Results may differ from the reference program's by a relative error of at most 0.0042.
Values may be sent and summed in bfloat16 or wider, within the bound.
No kernel may reach another device: no remote copies, remote signals or barrier semaphores. Data moves between devices by JAX's collectives and lax.ppermute only.
A program may use at most 128 MiB of HBM per device.

```python
import math
import jax
import jax.numpy as jnp
import numpy as np
from jax import lax

D = 4096
HEADS = 32
KVH = 8
HD = 128
EXPERTS = 8
FF = 8192
REQ = 4
FRESH = 32
PRIOR = 512
PAGE = 16
MAXP = 32
POOL = 128
TOK_G = 128
TOKENS = 8192
REQS = 256
CAP = 40
EXP_REP = 8
HIDREP = 1024
HIDDEV = 128
N_REP = 64
N_TP = 8


def drawn_draws(key):
    base = jax.random.fold_in(key, 11)
    blocks = TOKENS // FRESH
    group_size = HEADS // KVH
    kv_vals = jax.random.normal(jax.random.fold_in(base, 1), (blocks, FRESH, KVH, 2, HD), jnp.float32)
    query = jax.random.normal(jax.random.fold_in(base, 2), (blocks, FRESH, KVH, group_size, HD), jnp.float32)
    kv_vals = jnp.clip(kv_vals, -6.0, 6.0)
    query = jnp.clip(query, -6.0, 6.0)
    kv_vals = jnp.clip(kv_vals, -7.0, 7.0).reshape(TOKENS, KVH * 2 * HD)
    query = jnp.clip(query, -120.0, 120.0).reshape(TOKENS, HEADS * HD)
    return (query, kv_vals)


def draw_queries(key, part):
    return drawn_draws(key)[0].astype(jnp.bfloat16)


def draw_fresh_kv(key, part):
    return drawn_draws(key)[1].astype(jnp.bfloat16)


def draw_prior_len(key, part):
    basis = jax.random.randint(jax.random.fold_in(key, 21), (REQS,), PRIOR // 2, PRIOR + 1, dtype=jnp.int32)
    shifts = jax.random.randint(jax.random.fold_in(key, 22), (REQS,), 0, 4, dtype=jnp.int32)
    lengths = jnp.maximum(jnp.right_shift(basis, shifts), 1)
    spot = jax.random.randint(jax.random.fold_in(key, 23), (), 0, REQS, dtype=jnp.int32)
    return lengths.at[spot].set(PRIOR).astype(jnp.int32)


def draw_new_len(key, part):
    lengths = jax.random.randint(jax.random.fold_in(key, 31), (REQS,), FRESH // 2, FRESH + 1, dtype=jnp.int32)
    spot = jax.random.randint(jax.random.fold_in(key, 32), (), 0, REQS, dtype=jnp.int32)
    return lengths.at[spot].set(FRESH).astype(jnp.int32)


def set_ends(values, key, low, top_value):
    dims = values.shape
    index_at = [jax.random.randint(jax.random.fold_in(key, axis), (), 0, dims[axis]) for axis in range(len(dims))]
    values = values.at[tuple(index_at)].set(low)
    longest = dims.index(max(dims))
    index_at[longest] = (index_at[longest] + 1) % dims[longest]
    return values.at[tuple(index_at)].set(top_value)


def block_levels(key, extent, shards, least, largest):
    def one(position, shards_of):
        heights = jax.random.uniform(jax.random.fold_in(jax.random.fold_in(key, 6), position), (shards_of,), jnp.float32, least / len(shards), largest / len(shards))
        return jnp.repeat(jnp.exp(heights), extent[position] // shards_of).reshape((-1,) + (1,) * (len(extent) - position - 1))

    level = one(*shards[0])
    for cut in shards[1:]:
        level = level * one(*cut)
    return level


def routed_block(own_key, own, number, rows, amount, top, most, skew):
    ranking = jax.random.permutation(own_key, amount)
    packed, ordinary = portions_of(amount, rows * top, most, skew, True), portions_of(amount, rows * top, most, skew, False)
    places = jnp.arange(amount)

    def named(tallies, turn):
        used = int((tallies > 0).sum())
        fixed = max(1, used // 4)
        moved = fixed + (places - fixed + turn * (used - fixed)) % max(1, amount - fixed)
        return jnp.zeros((amount,), jnp.int32).at[ranking[jnp.where(places < fixed, places, moved)]].set(jnp.asarray(tallies, jnp.int32))

    tallies = jnp.where(number % 4 == 0, named(packed, number // 4), named(ordinary, number - number // 4 - 1))
    mixed = jax.random.permutation(jax.random.fold_in(own, 3), amount)
    giver, receiver = mixed[0:amount // 2 * 2:2], mixed[1:amount // 2 * 2:2]
    slack = jnp.minimum(tallies[giver] - 1, most - tallies[receiver]) // 2
    slack = jnp.where((giver == ranking[0]) | (receiver == ranking[0]) | (tallies[receiver] == 0), 0, jnp.maximum(slack, 0))
    moved = jax.random.randint(jax.random.fold_in(own, 4), (amount // 2,), 0, 1 << 20) % (slack + 1)
    tallies = tallies.at[giver].add(-moved).at[receiver].add(moved)
    items = jnp.searchsorted(jnp.cumsum(tallies), jnp.arange(rows * top), side="right").astype(jnp.int32)
    table = items.reshape(top, rows).T
    table = table[jax.random.permutation(jax.random.fold_in(own, 1), rows)]
    turn = jax.random.randint(jax.random.fold_in(own, 2), (rows, 1), 0, top)
    return jnp.take_along_axis(table, (jnp.arange(top)[None, :] + turn) % top, axis=1)


def portions_of(amount, total, bound, skew, full):
    weights = [(1 << 20) // math.isqrt(rank ** skew) + 1 for rank in range(1, amount + 1)]
    largest = bound if full else min(bound, max(-(-total // amount), total * weights[0] // sum(weights)))
    least = 1 if total - largest >= amount - 1 else 0
    given, surplus = [largest] + [least] * (amount - 1), total - largest - least * (amount - 1)
    while surplus > 0:
        candidates = [i for i in range(1, amount) if given[i] < largest] or [i for i in range(1, amount) if given[i] < bound]
        pool, budget = sum([weights[i] for i in candidates]), surplus
        for i in candidates:
            addition = min(bound - given[i], max(1, budget * weights[i] // pool), surplus)
            given[i] = given[i] + addition
            surplus = surplus - addition
    return np.array(given)


def centred(rng, shape, scale, reach, cuts=(), kind=jnp.bfloat16):
    values = scale * jax.random.normal(rng, shape, jnp.float32)
    if cuts:
        values = values * block_levels(rng, shape, cuts, -0.22, 0.18)
    return jnp.clip(values, -reach, reach).astype(kind)


def setup_inputs(seed: int = 0) -> dict:
    seeds = jax.random.split(jax.random.key(seed), 14)
    queries = draw_queries(jax.random.fold_in(seeds[13], 71), 0)
    fresh_kv = draw_fresh_kv(jax.random.fold_in(seeds[13], 71), 0)
    kv_pool = centred(seeds[2], (N_REP * POOL, PAGE, KVH * 2 * HD), 1.0, 6.0, ((0, 64), (2, 8)))
    residual = centred(seeds[3], (TOKENS, D), 1.0, 6.0, ((0, 64), (1, 8)))
    norm_gain = jnp.clip(1.0 + 0.18 * jax.random.normal(seeds[4], (D,), jnp.float32), 0.1, 1.9)
    gate_up = centred(seeds[5], (EXPERTS * EXP_REP, D, 2 * HIDREP), D ** -0.5, 0.09375, ((0, 64), (2, 8)))
    down_proj = centred(seeds[6], (EXPERTS * EXP_REP, HIDREP, D), FF ** -0.5, 0.0625, ((0, 64), (2, 8)))
    prior_len = draw_prior_len(jax.random.fold_in(seeds[13], 71), 0)
    new_len = draw_new_len(jax.random.fold_in(seeds[13], 71), 0)
    page_table = jax.vmap(lambda own: jax.random.permutation(own, POOL))(jax.random.split(seeds[9], N_REP)).reshape((N_REP, POOL)).astype(jnp.int32)
    leaving = set_ends(jax.random.randint(seeds[10], (N_REP,), 0, REQ), jax.random.fold_in(seeds[10], 1), 0, REQ - 1).astype(jnp.int32)
    expert_ids_keys = jax.random.split(jax.random.fold_in(seeds[11], 1), TOKENS // TOK_G)
    expert_ids_turns = jax.random.permutation(jax.random.fold_in(seeds[11], 3), TOKENS // TOK_G)
    expert_ids = jax.vmap(lambda own, number: routed_block(jax.random.fold_in(seeds[11], 2), own, number, TOK_G, EXPERTS, 2, CAP, 1))(expert_ids_keys, expert_ids_turns).reshape((TOKENS, 2))
    route_logits = centred(seeds[12], (TOKENS, 2), 1.0, 6.0, ((0, 64),), jnp.float32)
    return dict(queries=queries, fresh_kv=fresh_kv, kv_pool=kv_pool, residual=residual, norm_gain=norm_gain, gate_up=gate_up, down_proj=down_proj, prior_len=prior_len, new_len=new_len, page_table=page_table, leaving=leaving, expert_ids=expert_ids, route_logits=route_logits)


epsilon = 1e-05

def attend_one(query, keys, values, prior_count, new_count):
    group_size = HEADS // KVH
    grouped = query.reshape(FRESH, KVH, group_size, HD)
    scores = jnp.einsum('cgjd,kgd->gjck', grouped, keys) * HD ** (-0.5)
    key_pos = jnp.arange(PRIOR + FRESH, dtype=jnp.int32)
    key_offset = key_pos - PRIOR
    query_pos = jnp.arange(FRESH, dtype=jnp.int32)
    visible = jnp.where(key_pos[None, :] < PRIOR, key_pos[None, :] < prior_count, (key_offset[None, :] <= query_pos[:, None]) & (key_offset[None, :] < new_count))
    masked = jnp.where(visible, scores, -1e+30)
    highest = lax.optimization_barrier(jnp.max(masked, axis=-1, keepdims=True))
    expo = jnp.where(visible, jnp.exp(masked - highest), 0.0)
    totals = lax.optimization_barrier(jnp.sum(expo, axis=-1, keepdims=True))
    rounded = lax.optimization_barrier((expo / totals).astype(jnp.bfloat16))
    weights = rounded.astype(jnp.float32)
    mixed = jnp.einsum('gjck,kgd->cgjd', weights, values).reshape(FRESH, HEADS * HD)
    return jnp.where(query_pos[:, None] < new_count, mixed, 0.0).astype(jnp.bfloat16)

def reference(queries, fresh_kv, kv_pool, residual, norm_gain, gate_up, down_proj, prior_len, new_len, page_table, leaving, expert_ids, route_logits):
    tables = page_table.reshape(REQS, MAXP)

    def one_request(index):
        group_at = index // REQ
        pages = tables[index] + group_at * POOL
        earlier = kv_pool[pages].reshape(PRIOR, KVH, 2, HD).astype(jnp.float32)
        newer = lax.dynamic_slice_in_dim(fresh_kv, index * FRESH, FRESH, 0).reshape(FRESH, KVH, 2, HD).astype(jnp.float32)
        joined = jnp.concatenate([earlier, newer], axis=0)
        query = lax.dynamic_slice_in_dim(queries, index * FRESH, FRESH, 0).reshape(FRESH, HEADS, HD).astype(jnp.float32)
        return attend_one(query, joined[:, :, 0], joined[:, :, 1], prior_len[index], new_len[index])
    attn_old = lax.map(one_request, jnp.arange(REQS, dtype=jnp.int32))
    slot_ids = jnp.arange(REQS, dtype=jnp.int32)
    group_ids = slot_ids // REQ
    slot_in = slot_ids % REQ
    prev_group = (group_ids + N_REP - 1) % N_REP
    source = jnp.where(slot_in == leaving[group_ids], prev_group * REQ + leaving[prev_group], slot_ids)
    attention = attn_old[source].reshape(TOKENS, D)
    resid_new = residual.reshape(REQS, FRESH, D)[source].reshape(TOKENS, D)
    hidden = resid_new.astype(jnp.float32) + attention.astype(jnp.float32)
    scale = lax.rsqrt(lax.optimization_barrier(jnp.mean(hidden * hidden, axis=-1, keepdims=True)) + epsilon)
    normed = (hidden * scale * norm_gain[None, :]).astype(jnp.bfloat16)
    shares = jax.nn.softmax(route_logits, axis=-1)
    limit = N_REP * CAP

    def expert_step(running, expert):
        struck = expert_ids == expert
        routed = jnp.any(struck, axis=1)
        share_of = lax.optimization_barrier(jnp.sum(jnp.where(struck, shares, 0.0), axis=1))
        order = jnp.cumsum(routed.astype(jnp.int32)) - 1
        target = jnp.where(routed, order, limit)
        picks = jnp.zeros((limit,), jnp.int32).at[target].set(jnp.arange(TOKENS, dtype=jnp.int32), mode='drop')
        filled = jnp.arange(limit, dtype=jnp.int32) < jnp.sum(routed.astype(jnp.int32))
        rows_in = normed[picks]
        block = lax.dynamic_slice_in_dim(gate_up, expert * EXP_REP, EXP_REP, 0).reshape(EXP_REP, D, N_TP, 2, HIDDEV)
        block = jnp.transpose(block, (1, 3, 0, 2, 4)).reshape(D, 2, FF)
        gate_val = jnp.dot(rows_in, block[:, 0], preferred_element_type=jnp.float32)
        up_val = jnp.dot(rows_in, block[:, 1], preferred_element_type=jnp.float32)
        active = (jax.nn.silu(gate_val) * up_val).astype(jnp.bfloat16)
        downs = lax.dynamic_slice_in_dim(down_proj, expert * EXP_REP, EXP_REP, 0).reshape(FF, D)
        result = jnp.dot(active, downs, preferred_element_type=jnp.float32)
        factor = jnp.where(filled, share_of[picks], 0.0)
        return (running.at[picks].add(factor[:, None] * result), None)
    moe_out, _ = lax.scan(expert_step, jnp.zeros((TOKENS, D), jnp.float32), jnp.arange(EXPERTS, dtype=jnp.int32))
    return (hidden + moe_out).astype(jnp.bfloat16)
```

```python
import functools

import jax
import jax.numpy as jnp
from jax import lax
from jax.experimental import pallas as pl
from jax.experimental.pallas import tpu as pltpu
from jax.sharding import Mesh
from jax.sharding import PartitionSpec as P

D = 4096
HD = 128
EXPERTS = 8
REQ = 4
FRESH = 32
PRIOR = 512
PAGE = 16
CAP = 40

NX, NZ, NY, NC = 4, 16, 4, 2
N_REP = NX * NZ
N_TP = NY * NC
REP = ("x", "z")
TP = ("y", "c")
SPREAD = ("x", "y", "c")
SHARE = CAP // N_TP
PIECE = 2 * SHARE
ROWS = NX * PIECE
ALL_ROWS = NZ * ROWS
OWN_ROWS = ALL_ROWS // 2
WIDE = 640

epsilon = 1e-05


def attend_slots(query_rows, earlier, newer, prior_count, new_count):
    requests, fresh_len, q_width = query_rows.shape
    group_size = q_width // HD
    keys_all = jnp.concatenate([earlier, newer], axis=1)
    span_len = keys_all.shape[1]
    prior_span = earlier.shape[1]
    key_part = keys_all[:, :, :HD]
    value_part = keys_all[:, :, HD:]
    grouped = query_rows.reshape(requests, fresh_len, group_size, HD)
    scores = jnp.einsum(
        "rcjd,rkd->rjck", grouped, key_part, preferred_element_type=jnp.float32
    ) * HD ** (-0.5)
    key_pos = jnp.arange(span_len, dtype=jnp.int32)
    key_offset = key_pos - prior_span
    query_pos = jnp.arange(fresh_len, dtype=jnp.int32)
    visible = jnp.where(
        key_pos[None, None, :] < prior_span,
        key_pos[None, None, :] < prior_count[:, None, None],
        (key_offset[None, None, :] <= query_pos[None, :, None])
        & (key_offset[None, None, :] < new_count[:, None, None]),
    )
    visible = visible[:, None]
    masked = jnp.where(visible, scores, -1e30)
    highest = jnp.max(masked, axis=-1, keepdims=True)
    expo = jnp.where(visible, jnp.exp(masked - highest), 0.0)
    totals = jnp.sum(expo, axis=-1, keepdims=True)
    weights = (expo / totals).astype(jnp.bfloat16)
    mixed = jnp.einsum("rjck,rkd->rcjd", weights, value_part, preferred_element_type=jnp.float32)
    mixed = mixed.reshape(requests, fresh_len, q_width)
    return jnp.where(query_pos[None, :, None] < new_count[:, None, None], mixed, 0.0).astype(
        jnp.bfloat16
    )


def norm_kernel(recv_ref, out_ref, rows):
    for xs in range(NX):
        total = jnp.zeros((PIECE, 128), jnp.float32)
        for ts in range(N_TP):
            piece = recv_ref[xs * N_TP + ts].astype(jnp.float32)
            rows[xs * PIECE : (xs + 1) * PIECE, ts * 512 : (ts + 1) * 512] = piece[:, :512]
            total = total + piece[:, 512:]
        square = jnp.sum(total, axis=1, keepdims=True)
        scale = lax.rsqrt(square * (1.0 / D) + epsilon)
        here = slice(xs * PIECE, (xs + 1) * PIECE)
        rows[here, :] = rows[here, :] * scale
    out_ref[...] = rows[...].astype(jnp.bfloat16)


def norm_rows(received):
    return pl.pallas_call(
        norm_kernel,
        out_shape=jax.ShapeDtypeStruct((ROWS, D), jnp.bfloat16),
        scratch_shapes=[pltpu.VMEM((ROWS, D), jnp.float32)],
        name="norm_rows",
    )(received)


def expert_kernel(all_ref, take_ref, put_ref, in_ref, down_ref, out_ref, rows, active):
    step = pl.program_id(0)

    @pl.when(step == 0)
    def _():
        for n in range(8):
            part = slice(n * 512, (n + 1) * 512)
            rows[:, part] = jnp.dot(
                take_ref[...], all_ref[:, part], preferred_element_type=jnp.float32
            ).astype(jnp.bfloat16)

    @pl.when(step < N_TP)
    def _():
        both = jnp.dot(rows[...], in_ref[0], preferred_element_type=jnp.float32)
        gate = both[:, :128]
        value = (gate / (1.0 + jnp.exp(-gate)) * both[:, 128:]).astype(jnp.bfloat16)
        for t in range(N_TP):

            @pl.when(step == t)
            def _():
                active[:, t * 128 : (t + 1) * 128] = value

    @pl.when(step >= N_TP)
    def _():
        part = jnp.dot(active[...], down_ref[0], preferred_element_type=jnp.float32)
        out_ref[...] = jnp.dot(
            put_ref[...], part.astype(jnp.bfloat16), preferred_element_type=jnp.float32
        ).astype(jnp.bfloat16)


def run_experts(all_rows, take, put, weights_in, weights_down):
    last = N_TP - 1
    return pl.pallas_call(
        expert_kernel,
        out_shape=jax.ShapeDtypeStruct((ALL_ROWS, D), jnp.bfloat16),
        grid=(2 * N_TP,),
        in_specs=[
            pl.BlockSpec((ALL_ROWS, D), lambda j: (0, 0), pipeline_mode=pl.Buffered(1)),
            pl.BlockSpec((OWN_ROWS, ALL_ROWS), lambda j: (0, 0), pipeline_mode=pl.Buffered(1)),
            pl.BlockSpec((ALL_ROWS, OWN_ROWS), lambda j: (0, 0), pipeline_mode=pl.Buffered(1)),
            pl.BlockSpec((1, D, 256), lambda j: (jnp.minimum(j, last), 0, 0)),
            pl.BlockSpec((1, 1024, 512), lambda j: (jnp.maximum(j - N_TP, 0), 0, 0)),
        ],
        out_specs=pl.BlockSpec((ALL_ROWS, 512), lambda j: (0, jnp.maximum(j - N_TP, 0))),
        scratch_shapes=[
            pltpu.VMEM((OWN_ROWS, D), jnp.bfloat16),
            pltpu.VMEM((OWN_ROWS, 1024), jnp.bfloat16),
        ],
        compiler_params=pltpu.CompilerParams(
            dimension_semantics=("arbitrary",), vmem_limit_bytes=40 << 20
        ),
        name="experts",
    )(all_rows, take, put, weights_in, weights_down)


def three_parts(values):
    parts = []
    for _ in range(3):
        head = lax.reduce_precision(values, 8, 7)
        parts.append(head.astype(jnp.bfloat16))
        values = values - head
    return parts


def per_device(
    queries,
    fresh_kv,
    kv_pool,
    residual,
    norm_gain,
    gate_up,
    down_proj,
    prior_len,
    new_len,
    page_table,
    leaving,
    expert_ids,
    route_logits,
):
    my_z = lax.axis_index("z")
    my_group = lax.axis_index("x") * NZ + my_z
    leave_slot = leaving[my_group]
    handing = [(i, (i + 1) % N_REP) for i in range(N_REP)]

    weights_down = lax.all_gather(down_proj[0], TP)
    weights_in = lax.all_gather(gate_up[0], TP)

    query_heads = lax.all_to_all(queries, TP, split_axis=1, concat_axis=0, tiled=True)
    kv_rows = lax.all_to_all(fresh_kv, TP, split_axis=1, concat_axis=0, tiled=True)
    resid_slots = residual.reshape(REQ, FRESH, -1)
    resid_came = lax.ppermute(
        lax.dynamic_index_in_dim(resid_slots, leave_slot, 0, keepdims=False), REP, handing
    )
    tables = page_table[0].reshape(REQ, PRIOR // PAGE)
    earlier = kv_pool[tables].reshape(REQ, PRIOR, -1)
    own_prior = lax.dynamic_slice_in_dim(prior_len, my_group * REQ, REQ, 0)
    own_new = lax.dynamic_slice_in_dim(new_len, my_group * REQ, REQ, 0)
    attention = attend_slots(
        query_heads.reshape(REQ, FRESH, -1),
        earlier,
        kv_rows.reshape(REQ, FRESH, -1),
        own_prior,
        own_new,
    )
    attention_came = lax.ppermute(
        lax.dynamic_index_in_dim(attention, leave_slot, 0, keepdims=False), REP, handing
    )
    is_new = (jnp.arange(REQ, dtype=jnp.int32) == leave_slot)[:, None, None]
    resid_new = jnp.where(is_new, resid_came[None], resid_slots).astype(jnp.float32)
    attention_new = jnp.where(is_new, attention_came[None], attention).astype(jnp.float32)
    token_count = REQ * FRESH
    hidden = (resid_new + attention_new).reshape(token_count, -1)

    struck = (
        expert_ids[:, :, None] == jnp.arange(EXPERTS, dtype=jnp.int32)[None, None, :]
    ).astype(jnp.bfloat16)
    loads = struck[:, 0] + struck[:, 1]
    earlier_rows = (
        jnp.arange(token_count, dtype=jnp.int32)[:, None]
        > jnp.arange(token_count, dtype=jnp.int32)[None, :]
    ).astype(jnp.bfloat16)
    ahead = jnp.dot(earlier_rows, loads, preferred_element_type=jnp.float32)
    place = jnp.sum(struck.astype(jnp.float32) * ahead[:, None, :], axis=2).astype(jnp.int32)
    target = (
        ((expert_ids // 2) * N_TP + place // SHARE) * PIECE + (expert_ids % 2) * SHARE + place % SHARE
    )
    slots = jnp.arange(EXPERTS * CAP, dtype=jnp.int32)
    placing = (
        (target[:, 0][None, :] == slots[:, None]) | (target[:, 1][None, :] == slots[:, None])
    ).astype(jnp.bfloat16)

    squares = three_parts(jnp.sum(hidden * hidden, axis=1))
    extra = jnp.stack(squares + [jnp.zeros_like(squares[0])], axis=1)
    extra = jnp.pad(extra, ((0, 0), (0, WIDE - 512 - 4)))
    payload = jnp.concatenate(
        [(hidden * norm_gain[None, :]).astype(jnp.bfloat16), extra], axis=1
    )
    packed = jnp.dot(placing, payload, preferred_element_type=jnp.float32).astype(jnp.bfloat16)
    received = lax.all_to_all(packed.reshape(NX * N_TP, PIECE, WIDE), SPREAD, 0, 0)
    normed = norm_rows(received.reshape(NX * N_TP, PIECE, WIDE))
    all_rows = lax.all_gather(normed, "z", tiled=True)

    index = jnp.arange(ALL_ROWS, dtype=jnp.int32)
    own = (index // SHARE) % 2 == my_z // 8
    compact = jnp.where(own, (index // PIECE) * SHARE + index % SHARE, -1)
    own_index = jnp.arange(OWN_ROWS, dtype=jnp.int32)
    take = (own_index[:, None] == compact[None, :]).astype(jnp.bfloat16)
    put = (compact[:, None] == own_index[None, :]).astype(jnp.bfloat16)
    partial_rows = run_experts(all_rows, take, put, weights_in, weights_down)
    summed = lax.psum_scatter(partial_rows, "z", scatter_dimension=0, tiled=True)
    back = summed.reshape(NX, PIECE, N_TP, 512).transpose(0, 2, 1, 3)
    returned = lax.all_to_all(back.reshape(NX * N_TP, PIECE, 512), SPREAD, 0, 0)
    returned = returned.reshape(EXPERTS * CAP, 512)
    shares = jax.nn.softmax(route_logits, axis=-1)
    first = (target[:, 0][:, None] == slots[None, :]).astype(jnp.bfloat16)
    second = (target[:, 1][:, None] == slots[None, :]).astype(jnp.bfloat16)
    moe_out = shares[:, 0:1] * jnp.dot(
        first, returned, preferred_element_type=jnp.float32
    ) + shares[:, 1:2] * jnp.dot(second, returned, preferred_element_type=jnp.float32)
    return (hidden + moe_out).astype(jnp.bfloat16)


def solution(mesh):
    inner = Mesh(mesh.devices.reshape(NX, NZ, NY, NC), ("x", "z", "y", "c"))
    every = ("x", "z", "y", "c")
    in_specs = (
        P(every, None),
        P(every, None),
        P(REP, None, TP),
        P(REP, TP),
        P(TP),
        P(REP, None, TP),
        P(REP, None, TP),
        P(),
        P(),
        P(REP, None),
        P(),
        P(REP, None),
        P(REP, None),
    )
    return jax.shard_map(
        per_device, mesh=inner, in_specs=in_specs, out_specs=P(REP, TP), check_vma=False
    )
```

```python
import functools

import jax
import jax.numpy as jnp
from jax import lax
from jax.experimental import pallas as pl
from jax.experimental.pallas import tpu as pltpu
from jax.sharding import Mesh
from jax.sharding import PartitionSpec as P

D = 4096
HD = 128
EXPERTS = 8
REQ = 4
FRESH = 32
PRIOR = 512
PAGE = 16
CAP = 40

NX, NZ, NY, NC = 4, 16, 4, 2
N_REP = NX * NZ
N_TP = NY * NC
REP = ("x", "z")
TP = ("y", "c")
SPREAD = ("x", "y", "c")
SHARE = CAP // N_TP
PIECE = 2 * SHARE
ROWS = NX * PIECE
ALL_ROWS = NZ * ROWS
OWN_ROWS = ALL_ROWS // 2
WIDE = 640

epsilon = 1e-05


def attend_slots(query_rows, earlier, newer, prior_count, new_count):
    requests, fresh_len, q_width = query_rows.shape
    group_size = q_width // HD
    keys_all = jnp.concatenate([earlier, newer], axis=1)
    span_len = keys_all.shape[1]
    prior_span = earlier.shape[1]
    key_part = keys_all[:, :, :HD]
    value_part = keys_all[:, :, HD:]
    grouped = query_rows.reshape(requests, fresh_len, group_size, HD)
    scores = jnp.einsum(
        "rcjd,rkd->rjck", grouped, key_part, preferred_element_type=jnp.float32
    ) * HD ** (-0.5)
    key_pos = jnp.arange(span_len, dtype=jnp.int32)
    key_offset = key_pos - prior_span
    query_pos = jnp.arange(fresh_len, dtype=jnp.int32)
    visible = jnp.where(
        key_pos[None, None, :] < prior_span,
        key_pos[None, None, :] < prior_count[:, None, None],
        (key_offset[None, None, :] <= query_pos[None, :, None])
        & (key_offset[None, None, :] < new_count[:, None, None]),
    )
    visible = visible[:, None]
    masked = jnp.where(visible, scores, -1e30)
    highest = jnp.max(masked, axis=-1, keepdims=True)
    expo = jnp.where(visible, jnp.exp(masked - highest), 0.0)
    totals = jnp.sum(expo, axis=-1, keepdims=True)
    weights = (expo / totals).astype(jnp.bfloat16)
    mixed = jnp.einsum("rjck,rkd->rcjd", weights, value_part, preferred_element_type=jnp.float32)
    mixed = mixed.reshape(requests, fresh_len, q_width)
    return jnp.where(query_pos[None, :, None] < new_count[:, None, None], mixed, 0.0).astype(
        jnp.bfloat16
    )


def norm_kernel(recv_ref, out_ref, rows):
    for xs in range(NX):
        total = jnp.zeros((PIECE, 128), jnp.float32)
        for ts in range(N_TP):
            piece = recv_ref[xs * N_TP + ts].astype(jnp.float32)
            rows[xs * PIECE : (xs + 1) * PIECE, ts * 512 : (ts + 1) * 512] = piece[:, :512]
            total = total + piece[:, 512:]
        square = jnp.sum(total, axis=1, keepdims=True)
        scale = lax.rsqrt(square * (1.0 / D) + epsilon)
        here = slice(xs * PIECE, (xs + 1) * PIECE)
        rows[here, :] = rows[here, :] * scale
    out_ref[...] = rows[...].astype(jnp.bfloat16)


def norm_rows(received):
    return pl.pallas_call(
        norm_kernel,
        out_shape=jax.ShapeDtypeStruct((ROWS, D), jnp.bfloat16),
        scratch_shapes=[pltpu.VMEM((ROWS, D), jnp.float32)],
        name="norm_rows",
    )(received)


def expert_kernel(order_ref, all_ref, take_ref, put_ref, *refs):
    in_refs, down_refs = refs[:10], refs[10:20]
    out_ref, gathered, rows, in_buf, down_buf, active, whole, parts, sems = refs[20:]
    copies = [[pltpu.make_async_copy(all_ref, gathered, sems.at[0])]]
    count = 1
    for pieces, buf in ((in_refs, in_buf), (down_refs, down_buf)):
        for core in range(2):
            for k in range(4):
                chunk = buf.at[core * 4 + k]
                found = []
                if k < 3:
                    found.append((pieces[core * 5 + k], chunk))
                else:
                    half = chunk.shape[0] // 2
                    found.append((pieces[core * 5 + 3], chunk.at[pl.ds(0, half)]))
                    found.append((pieces[core * 5 + 4], chunk.at[pl.ds(half, half)]))
                group = []
                for source, target in found:
                    group.append(pltpu.make_async_copy(source, target, sems.at[count]))
                    count += 1
                copies.append(group)
    for group in copies:
        for copy in group:
            copy.start()
    copies[0][0].wait()
    for n in range(8):
        part = slice(n * 512, (n + 1) * 512)
        rows[:, part] = jnp.dot(
            take_ref[...], gathered[:, part], preferred_element_type=jnp.float32
        ).astype(jnp.bfloat16)
    for k in range(N_TP):
        for copy in copies[1 + k]:
            copy.wait()
        both = jnp.dot(rows[...], in_buf[k], preferred_element_type=jnp.float32)
        gate = both[:, :128]
        active[order_ref[k]] = (gate / (1.0 + jnp.exp(-gate)) * both[:, 128:]).astype(jnp.bfloat16)
    for t in range(N_TP):
        whole[:, t * 128 : (t + 1) * 128] = active[t]
    outs = []
    for k in range(N_TP):
        for copy in copies[1 + N_TP + k]:
            copy.wait()
        part = jnp.dot(whole[...], down_buf[k], preferred_element_type=jnp.float32)
        parts[k] = jnp.dot(
            put_ref[...], part.astype(jnp.bfloat16), preferred_element_type=jnp.float32
        ).astype(jnp.bfloat16)
        lanes = pl.ds(pl.multiple_of(order_ref[k] * 512, 512), 512)
        copy = pltpu.make_async_copy(parts.at[k], out_ref.at[:, lanes], sems.at[count])
        count += 1
        copy.start()
        outs.append(copy)
    for copy in outs:
        copy.wait()


def run_experts(order, all_rows, take, put, weights_in, weights_down):
    anywhere = pl.BlockSpec(memory_space=pl.ANY)
    local = pl.BlockSpec(memory_space=pltpu.VMEM)
    return pl.pallas_call(
        expert_kernel,
        out_shape=jax.ShapeDtypeStruct((ALL_ROWS, D), jnp.bfloat16),
        in_specs=[pl.BlockSpec(memory_space=pltpu.SMEM), anywhere, local, local] + [anywhere] * 20,
        out_specs=anywhere,
        scratch_shapes=[
            pltpu.VMEM((ALL_ROWS, D), jnp.bfloat16),
            pltpu.VMEM((OWN_ROWS, D), jnp.bfloat16),
            pltpu.VMEM((N_TP, D, 256), jnp.bfloat16),
            pltpu.VMEM((N_TP, 1024, 512), jnp.bfloat16),
            pltpu.VMEM((N_TP, OWN_ROWS, 128), jnp.bfloat16),
            pltpu.VMEM((OWN_ROWS, 1024), jnp.bfloat16),
            pltpu.VMEM((N_TP, ALL_ROWS, 512), jnp.bfloat16),
            pltpu.SemaphoreType.DMA((29,)),
        ],
        compiler_params=pltpu.CompilerParams(vmem_limit_bytes=50 << 20),
        name="experts",
    )(order, all_rows, take, put, *weights_in, *weights_down)


def by_y(value, step):
    return lax.ppermute(value, "y", [(i, (i + step) % NY) for i in range(NY)])


def other_core(value):
    return lax.ppermute(value, "c", [(0, 1), (1, 0)])


def gather_rest(own, below, above):
    half = own.shape[0] // 2
    pieces = [own, below, above, by_y(below[:half], 1), by_y(above[half:], -1)]
    return pieces + [other_core(piece) for piece in pieces]


def three_parts(values):
    parts = []
    for _ in range(3):
        head = lax.reduce_precision(values, 8, 7)
        parts.append(head.astype(jnp.bfloat16))
        values = values - head
    return parts


def per_device(
    queries,
    fresh_kv,
    kv_pool,
    residual,
    norm_gain,
    gate_up,
    down_proj,
    prior_len,
    new_len,
    page_table,
    leaving,
    expert_ids,
    route_logits,
):
    my_z = lax.axis_index("z")
    my_group = lax.axis_index("x") * NZ + my_z
    leave_slot = leaving[my_group]
    handing = [(i, (i + 1) % N_REP) for i in range(N_REP)]

    in_own, down_own = gate_up[0], down_proj[0]
    mixed = jnp.concatenate(
        [queries.reshape(-1, N_TP, 512), fresh_kv.reshape(-1, N_TP, 256)], axis=2
    )
    heads = lax.all_to_all(mixed, TP, split_axis=1, concat_axis=0, tiled=True)[:, 0]
    query_heads, kv_rows = heads[:, :512], heads[:, 512:]
    in_below, in_above = by_y(in_own, 1), by_y(in_own, -1)
    resid_slots = residual.reshape(REQ, FRESH, -1)
    resid_came = lax.ppermute(
        lax.dynamic_index_in_dim(resid_slots, leave_slot, 0, keepdims=False), REP, handing
    )
    tables = page_table[0].reshape(REQ, PRIOR // PAGE)
    earlier = kv_pool[tables].reshape(REQ, PRIOR, -1)
    own_prior = lax.dynamic_slice_in_dim(prior_len, my_group * REQ, REQ, 0)
    own_new = lax.dynamic_slice_in_dim(new_len, my_group * REQ, REQ, 0)
    attention = attend_slots(
        query_heads.reshape(REQ, FRESH, -1),
        earlier,
        kv_rows.reshape(REQ, FRESH, -1),
        own_prior,
        own_new,
    )
    attention_came = lax.ppermute(
        lax.dynamic_index_in_dim(attention, leave_slot, 0, keepdims=False), REP, handing
    )
    is_new = (jnp.arange(REQ, dtype=jnp.int32) == leave_slot)[:, None, None]
    resid_new = jnp.where(is_new, resid_came[None], resid_slots).astype(jnp.float32)
    attention_new = jnp.where(is_new, attention_came[None], attention).astype(jnp.float32)
    token_count = REQ * FRESH
    hidden = (resid_new + attention_new).reshape(token_count, -1)

    struck = (
        expert_ids[:, :, None] == jnp.arange(EXPERTS, dtype=jnp.int32)[None, None, :]
    ).astype(jnp.bfloat16)
    loads = struck[:, 0] + struck[:, 1]
    earlier_rows = (
        jnp.arange(token_count, dtype=jnp.int32)[:, None]
        > jnp.arange(token_count, dtype=jnp.int32)[None, :]
    ).astype(jnp.bfloat16)
    ahead = jnp.dot(earlier_rows, loads, preferred_element_type=jnp.float32)
    place = jnp.sum(struck.astype(jnp.float32) * ahead[:, None, :], axis=2).astype(jnp.int32)
    target = (
        ((expert_ids // 2) * N_TP + place // SHARE) * PIECE + (expert_ids % 2) * SHARE + place % SHARE
    )
    slots = jnp.arange(EXPERTS * CAP, dtype=jnp.int32)
    placing = (
        (target[:, 0][None, :] == slots[:, None]) | (target[:, 1][None, :] == slots[:, None])
    ).astype(jnp.bfloat16)

    squares = three_parts(jnp.sum(hidden * hidden, axis=1))
    extra = jnp.stack(squares + [jnp.zeros_like(squares[0])], axis=1)
    extra = jnp.pad(extra, ((0, 0), (0, WIDE - 512 - 4)))
    payload = jnp.concatenate(
        [(hidden * norm_gain[None, :]).astype(jnp.bfloat16), extra], axis=1
    )
    packed = jnp.dot(placing, payload, preferred_element_type=jnp.float32).astype(jnp.bfloat16)
    received = lax.all_to_all(packed.reshape(NX * N_TP, PIECE, WIDE), SPREAD, 0, 0)
    normed = norm_rows(received.reshape(NX * N_TP, PIECE, WIDE))
    normed, in_own, in_below, in_above, down_own = lax.optimization_barrier(
        (normed, in_own, in_below, in_above, down_own)
    )
    all_rows = lax.all_gather(normed, "z", tiled=True)
    weights_in = gather_rest(in_own, in_below, in_above)
    weights_down = gather_rest(down_own, by_y(down_own, 1), by_y(down_own, -1))
    my_y, my_core = lax.axis_index("y"), lax.axis_index("c")
    piece = jnp.arange(N_TP, dtype=jnp.int32)
    step = piece % 4
    step = jnp.where(step == 1, NY - 1, jnp.where(step == 2, 1, jnp.where(step == 3, 2, 0)))
    order = (my_y + step) % NY * NC + (my_core + piece // 4) % NC

    index = jnp.arange(ALL_ROWS, dtype=jnp.int32)
    own = (index // SHARE) % 2 == my_z // 8
    compact = jnp.where(own, (index // PIECE) * SHARE + index % SHARE, -1)
    own_index = jnp.arange(OWN_ROWS, dtype=jnp.int32)
    take = (own_index[:, None] == compact[None, :]).astype(jnp.bfloat16)
    put = (compact[:, None] == own_index[None, :]).astype(jnp.bfloat16)
    partial_rows = run_experts(order, all_rows, take, put, weights_in, weights_down)
    summed = lax.psum_scatter(partial_rows, "z", scatter_dimension=0, tiled=True)
    back = summed.reshape(NX, PIECE, N_TP, 512).transpose(0, 2, 1, 3)
    returned = lax.all_to_all(back.reshape(NX * N_TP, PIECE, 512), SPREAD, 0, 0)
    returned = returned.reshape(EXPERTS * CAP, 512)
    shares = jax.nn.softmax(route_logits, axis=-1)
    first = (target[:, 0][:, None] == slots[None, :]).astype(jnp.bfloat16)
    second = (target[:, 1][:, None] == slots[None, :]).astype(jnp.bfloat16)
    moe_out = shares[:, 0:1] * jnp.dot(
        first, returned, preferred_element_type=jnp.float32
    ) + shares[:, 1:2] * jnp.dot(second, returned, preferred_element_type=jnp.float32)
    return (hidden + moe_out).astype(jnp.bfloat16)


def solution(mesh):
    inner = Mesh(mesh.devices.reshape(NX, NZ, NY, NC), ("x", "z", "y", "c"))
    every = ("x", "z", "y", "c")
    in_specs = (
        P(every, None),
        P(every, None),
        P(REP, None, TP),
        P(REP, TP),
        P(TP),
        P(REP, None, TP),
        P(REP, None, TP),
        P(),
        P(),
        P(REP, None),
        P(),
        P(REP, None),
        P(REP, None),
    )
    return jax.shard_map(
        per_device, mesh=inner, in_specs=in_specs, out_specs=P(REP, TP), check_vma=False
    )
```

```python
import functools

import jax
import jax.numpy as jnp
from jax import lax
from jax.experimental import pallas as pl
from jax.experimental.pallas import tpu as pltpu
from jax.sharding import Mesh
from jax.sharding import PartitionSpec as P

D = 4096
HD = 128
EXPERTS = 8
REQ = 4
FRESH = 32
PRIOR = 512
PAGE = 16
CAP = 40

NX, NZ, NY, NC = 4, 16, 4, 2
N_REP = NX * NZ
N_TP = NY * NC
REP = ("x", "z")
TP = ("y", "c")
SPREAD = ("x", "y", "c")
SHARE = CAP // N_TP
PIECE = 2 * SHARE
ROWS = NX * PIECE
ALL_ROWS = NZ * ROWS
OWN_ROWS = ALL_ROWS // 2
WIDE = 640

epsilon = 1e-05


def attend_slots(query_rows, earlier, newer, prior_count, new_count):
    requests, fresh_len, q_width = query_rows.shape
    group_size = q_width // HD
    keys_all = jnp.concatenate([earlier, newer], axis=1)
    span_len = keys_all.shape[1]
    prior_span = earlier.shape[1]
    key_part = keys_all[:, :, :HD]
    value_part = keys_all[:, :, HD:]
    grouped = query_rows.reshape(requests, fresh_len, group_size, HD)
    scores = jnp.einsum(
        "rcjd,rkd->rjck", grouped, key_part, preferred_element_type=jnp.float32
    ) * HD ** (-0.5)
    key_pos = jnp.arange(span_len, dtype=jnp.int32)
    key_offset = key_pos - prior_span
    query_pos = jnp.arange(fresh_len, dtype=jnp.int32)
    visible = jnp.where(
        key_pos[None, None, :] < prior_span,
        key_pos[None, None, :] < prior_count[:, None, None],
        (key_offset[None, None, :] <= query_pos[None, :, None])
        & (key_offset[None, None, :] < new_count[:, None, None]),
    )
    visible = visible[:, None]
    masked = jnp.where(visible, scores, -1e30)
    highest = jnp.max(masked, axis=-1, keepdims=True)
    expo = jnp.where(visible, jnp.exp(masked - highest), 0.0)
    totals = jnp.sum(expo, axis=-1, keepdims=True)
    weights = (expo / totals).astype(jnp.bfloat16)
    mixed = jnp.einsum("rjck,rkd->rcjd", weights, value_part, preferred_element_type=jnp.float32)
    mixed = mixed.reshape(requests, fresh_len, q_width)
    return jnp.where(query_pos[None, :, None] < new_count[:, None, None], mixed, 0.0).astype(
        jnp.bfloat16
    )


def norm_kernel(recv_ref, out_ref, rows):
    for xs in range(NX):
        total = jnp.zeros((PIECE, 128), jnp.float32)
        for ts in range(N_TP):
            piece = recv_ref[xs * N_TP + ts].astype(jnp.float32)
            rows[xs * PIECE : (xs + 1) * PIECE, ts * 512 : (ts + 1) * 512] = piece[:, :512]
            total = total + piece[:, 512:]
        square = jnp.sum(total, axis=1, keepdims=True)
        scale = lax.rsqrt(square * (1.0 / D) + epsilon)
        here = slice(xs * PIECE, (xs + 1) * PIECE)
        rows[here, :] = rows[here, :] * scale
    out_ref[...] = rows[...].astype(jnp.bfloat16)


def norm_rows(received):
    return pl.pallas_call(
        norm_kernel,
        out_shape=jax.ShapeDtypeStruct((ROWS, D), jnp.bfloat16),
        scratch_shapes=[pltpu.VMEM((ROWS, D), jnp.float32)],
        name="norm_rows",
    )(received)


CHUNKS = 4


def expert_kernel(order_ref, all_ref, take_ref, put_ref, *refs):
    in_refs, down_hbm = refs[:14], refs[14]
    out_ref, gathered, rows, in_buf, down_buf, active, whole, sems = refs[15:]
    width = D // CHUNKS
    half = D // 2
    count = iter(range(30))

    def begin(source, target):
        copy = pltpu.make_async_copy(source, target, sems.at[next(count)])
        copy.start()
        return copy

    parts = [
        begin(all_ref.at[:, pl.ds(n * width, width)], gathered.at[n]) for n in range(CHUNKS)
    ]
    loads = []
    for core in range(NC):
        for k in range(NY):
            chunk, first = in_buf.at[core * NY + k], core * 7 + 2 * k
            if k == 0:
                loads.append([begin(in_refs[first], chunk)])
            else:
                loads.append(
                    [
                        begin(in_refs[first - 1], chunk.at[pl.ds(0, half)]),
                        begin(in_refs[first], chunk.at[pl.ds(half, half)]),
                    ]
                )
    downs = [begin(down_hbm.at[t], down_buf.at[t]) for t in range(N_TP)]
    for n in range(CHUNKS):
        parts[n].wait()
        rows[:, n * width : (n + 1) * width] = jnp.dot(
            take_ref[...], gathered[n], preferred_element_type=jnp.float32
        ).astype(jnp.bfloat16)
    for k in range(N_TP):
        for copy in loads[k]:
            copy.wait()
        both = jnp.dot(rows[...], in_buf[k], preferred_element_type=jnp.float32)
        gate = both[:, :128]
        active[order_ref[k]] = (gate / (1.0 + jnp.exp(-gate)) * both[:, 128:]).astype(jnp.bfloat16)
    for t in range(N_TP):
        whole[:, t * 128 : (t + 1) * 128] = active[t]
    outs = []
    for t in range(N_TP):
        downs[t].wait()
        part = jnp.dot(whole[...], down_buf[t], preferred_element_type=jnp.float32)
        n, lane = t // 2, t % 2 * 512
        gathered[n, :, lane : lane + 512] = jnp.dot(
            put_ref[...], part.astype(jnp.bfloat16), preferred_element_type=jnp.float32
        ).astype(jnp.bfloat16)
        if t % 2:
            outs.append(begin(gathered.at[n], out_ref.at[:, pl.ds(n * width, width)]))
    for copy in outs:
        copy.wait()


def run_experts(order, all_rows, take, put, weights_in, weights_down):
    far = pl.BlockSpec(memory_space=pltpu.HBM)
    local = pl.BlockSpec(memory_space=pltpu.VMEM)
    return pl.pallas_call(
        expert_kernel,
        out_shape=jax.ShapeDtypeStruct((ALL_ROWS, D), jnp.bfloat16),
        in_specs=[pl.BlockSpec(memory_space=pltpu.SMEM), far, local, local] + [far] * 15,
        out_specs=far,
        scratch_shapes=[
            pltpu.VMEM((CHUNKS, ALL_ROWS, D // CHUNKS), jnp.bfloat16),
            pltpu.VMEM((OWN_ROWS, D), jnp.bfloat16),
            pltpu.VMEM((N_TP, D, 256), jnp.bfloat16),
            pltpu.VMEM((N_TP, 1024, 512), jnp.bfloat16),
            pltpu.VMEM((N_TP, OWN_ROWS, 128), jnp.bfloat16),
            pltpu.VMEM((OWN_ROWS, 1024), jnp.bfloat16),
            pltpu.SemaphoreType.DMA((30,)),
        ],
        compiler_params=pltpu.CompilerParams(vmem_limit_bytes=46 << 20),
        name="experts",
    )(order, all_rows, take, put, *weights_in, weights_down)


def by_y(value, step):
    return lax.ppermute(value, "y", [(i, (i + step) % NY) for i in range(NY)])


def other_core(value):
    return lax.ppermute(value, "c", [(0, 1), (1, 0)])


def gather_pieces(own):
    half = own.shape[0] // 2
    top, bottom = own[:half], own[half:]
    below_top, above_bottom = by_y(top, 1), by_y(bottom, -1)
    below_bottom, above_top = by_y(bottom, 1), by_y(top, -1)
    far_top, far_bottom = by_y(below_top, 1), by_y(above_bottom, -1)
    pieces = [own, below_top, below_bottom, above_top, above_bottom, far_top, far_bottom]
    return pieces + [other_core(piece) for piece in pieces]


def three_parts(values):
    parts = []
    for _ in range(3):
        head = lax.reduce_precision(values, 8, 7)
        parts.append(head.astype(jnp.bfloat16))
        values = values - head
    return parts


def per_device(
    queries,
    fresh_kv,
    kv_pool,
    residual,
    norm_gain,
    gate_up,
    down_proj,
    prior_len,
    new_len,
    page_table,
    leaving,
    expert_ids,
    route_logits,
):
    my_z = lax.axis_index("z")
    my_group = lax.axis_index("x") * NZ + my_z
    leave_slot = leaving[my_group]
    handing = [(i, (i + 1) % N_REP) for i in range(N_REP)]

    in_own = gate_up[0]
    weights_down = lax.all_gather(down_proj[0], TP)
    mixed = jnp.concatenate(
        [queries.reshape(-1, N_TP, 512), fresh_kv.reshape(-1, N_TP, 256)], axis=2
    )
    heads = lax.all_to_all(mixed, TP, split_axis=1, concat_axis=0, tiled=True)[:, 0]
    query_heads, kv_rows = heads[:, :512], heads[:, 512:]
    resid_slots = residual.reshape(REQ, FRESH, -1)
    resid_came = lax.ppermute(
        lax.dynamic_index_in_dim(resid_slots, leave_slot, 0, keepdims=False), REP, handing
    )
    tables = page_table[0].reshape(REQ, PRIOR // PAGE)
    earlier = kv_pool[tables].reshape(REQ, PRIOR, -1)
    own_prior = lax.dynamic_slice_in_dim(prior_len, my_group * REQ, REQ, 0)
    own_new = lax.dynamic_slice_in_dim(new_len, my_group * REQ, REQ, 0)
    attention = attend_slots(
        query_heads.reshape(REQ, FRESH, -1),
        earlier,
        kv_rows.reshape(REQ, FRESH, -1),
        own_prior,
        own_new,
    )
    attention_came = lax.ppermute(
        lax.dynamic_index_in_dim(attention, leave_slot, 0, keepdims=False), REP, handing
    )
    is_new = (jnp.arange(REQ, dtype=jnp.int32) == leave_slot)[:, None, None]
    resid_new = jnp.where(is_new, resid_came[None], resid_slots).astype(jnp.float32)
    attention_new = jnp.where(is_new, attention_came[None], attention).astype(jnp.float32)
    token_count = REQ * FRESH
    hidden = (resid_new + attention_new).reshape(token_count, -1)

    struck = (
        expert_ids[:, :, None] == jnp.arange(EXPERTS, dtype=jnp.int32)[None, None, :]
    ).astype(jnp.bfloat16)
    loads = struck[:, 0] + struck[:, 1]
    earlier_rows = (
        jnp.arange(token_count, dtype=jnp.int32)[:, None]
        > jnp.arange(token_count, dtype=jnp.int32)[None, :]
    ).astype(jnp.bfloat16)
    ahead = jnp.dot(earlier_rows, loads, preferred_element_type=jnp.float32)
    place = jnp.sum(struck.astype(jnp.float32) * ahead[:, None, :], axis=2).astype(jnp.int32)
    target = (
        ((expert_ids // 2) * N_TP + place // SHARE) * PIECE + (expert_ids % 2) * SHARE + place % SHARE
    )
    slots = jnp.arange(EXPERTS * CAP, dtype=jnp.int32)
    placing = (
        (target[:, 0][None, :] == slots[:, None]) | (target[:, 1][None, :] == slots[:, None])
    ).astype(jnp.bfloat16)

    squares = three_parts(jnp.sum(hidden * hidden, axis=1))
    extra = jnp.stack(squares + [jnp.zeros_like(squares[0])], axis=1)
    extra = jnp.pad(extra, ((0, 0), (0, WIDE - 512 - 4)))
    payload = jnp.concatenate(
        [(hidden * norm_gain[None, :]).astype(jnp.bfloat16), extra], axis=1
    )
    packed = jnp.dot(placing, payload, preferred_element_type=jnp.float32).astype(jnp.bfloat16)
    received = lax.all_to_all(packed.reshape(NX * N_TP, PIECE, WIDE), SPREAD, 0, 0)
    normed = norm_rows(received.reshape(NX * N_TP, PIECE, WIDE))
    normed, in_own, weights_down = lax.optimization_barrier((normed, in_own, weights_down))
    all_rows = lax.all_gather(normed, "z", tiled=True)
    weights_in = gather_pieces(in_own)
    my_y, my_core = lax.axis_index("y"), lax.axis_index("c")
    piece = jnp.arange(N_TP, dtype=jnp.int32)
    step = piece % 4
    step = jnp.where(step == 1, NY - 1, jnp.where(step == 2, 1, jnp.where(step == 3, 2, 0)))
    order = (my_y + step) % NY * NC + (my_core + piece // 4) % NC

    index = jnp.arange(ALL_ROWS, dtype=jnp.int32)
    own = (index // SHARE) % 2 == my_z // 8
    compact = jnp.where(own, (index // PIECE) * SHARE + index % SHARE, -1)
    own_index = jnp.arange(OWN_ROWS, dtype=jnp.int32)
    take = (own_index[:, None] == compact[None, :]).astype(jnp.bfloat16)
    put = (compact[:, None] == own_index[None, :]).astype(jnp.bfloat16)
    partial_rows = run_experts(order, all_rows, take, put, weights_in, weights_down)
    summed = lax.psum_scatter(partial_rows, "z", scatter_dimension=0, tiled=True)
    back = summed.reshape(NX, PIECE, N_TP, 512).transpose(0, 2, 1, 3)
    returned = lax.all_to_all(back.reshape(NX * N_TP, PIECE, 512), SPREAD, 0, 0)
    returned = returned.reshape(EXPERTS * CAP, 512)
    shares = jax.nn.softmax(route_logits, axis=-1)
    first = (target[:, 0][:, None] == slots[None, :]).astype(jnp.bfloat16)
    second = (target[:, 1][:, None] == slots[None, :]).astype(jnp.bfloat16)
    moe_out = shares[:, 0:1] * jnp.dot(
        first, returned, preferred_element_type=jnp.float32
    ) + shares[:, 1:2] * jnp.dot(second, returned, preferred_element_type=jnp.float32)
    return (hidden + moe_out).astype(jnp.bfloat16)


def solution(mesh):
    inner = Mesh(mesh.devices.reshape(NX, NZ, NY, NC), ("x", "z", "y", "c"))
    every = ("x", "z", "y", "c")
    in_specs = (
        P(every, None),
        P(every, None),
        P(REP, None, TP),
        P(REP, TP),
        P(TP),
        P(REP, None, TP),
        P(REP, None, TP),
        P(),
        P(),
        P(REP, None),
        P(),
        P(REP, None),
        P(REP, None),
    )
    return jax.shard_map(
        per_device, mesh=inner, in_specs=in_specs, out_specs=P(REP, TP), check_vma=False
    )
```

```python
import functools

import jax
import jax.numpy as jnp
from jax import lax
from jax.experimental import pallas as pl
from jax.experimental.pallas import tpu as pltpu
from jax.sharding import Mesh
from jax.sharding import PartitionSpec as P

D = 4096
HD = 128
EXPERTS = 8
REQ = 4
FRESH = 32
PRIOR = 512
PAGE = 16
CAP = 40

NX, NZ, NY, NC = 4, 16, 4, 2
N_REP = NX * NZ
N_TP = NY * NC
REP = ("x", "z")
TP = ("y", "c")
SPREAD = ("x", "y", "c")
SHARE = CAP // N_TP
PIECE = 2 * SHARE
ROWS = NX * PIECE
ALL_ROWS = NZ * ROWS
OWN_ROWS = ALL_ROWS // 2
WIDE = 640

epsilon = 1e-05


def attend_slots(query_rows, earlier, newer, prior_count, new_count):
    requests, fresh_len, q_width = query_rows.shape
    group_size = q_width // HD
    keys_all = jnp.concatenate([earlier, newer], axis=1)
    span_len = keys_all.shape[1]
    prior_span = earlier.shape[1]
    key_part = keys_all[:, :, :HD]
    value_part = keys_all[:, :, HD:]
    grouped = query_rows.reshape(requests, fresh_len, group_size, HD)
    scores = jnp.einsum(
        "rcjd,rkd->rjck", grouped, key_part, preferred_element_type=jnp.float32
    ) * HD ** (-0.5)
    key_pos = jnp.arange(span_len, dtype=jnp.int32)
    key_offset = key_pos - prior_span
    query_pos = jnp.arange(fresh_len, dtype=jnp.int32)
    visible = jnp.where(
        key_pos[None, None, :] < prior_span,
        key_pos[None, None, :] < prior_count[:, None, None],
        (key_offset[None, None, :] <= query_pos[None, :, None])
        & (key_offset[None, None, :] < new_count[:, None, None]),
    )
    visible = visible[:, None]
    masked = jnp.where(visible, scores, -1e30)
    highest = jnp.max(masked, axis=-1, keepdims=True)
    expo = jnp.where(visible, jnp.exp(masked - highest), 0.0)
    totals = jnp.sum(expo, axis=-1, keepdims=True)
    weights = (expo / totals).astype(jnp.bfloat16)
    mixed = jnp.einsum("rjck,rkd->rcjd", weights, value_part, preferred_element_type=jnp.float32)
    mixed = mixed.reshape(requests, fresh_len, q_width)
    return jnp.where(query_pos[None, :, None] < new_count[:, None, None], mixed, 0.0).astype(
        jnp.bfloat16
    )


def norm_kernel(recv_ref, out_ref, rows):
    for xs in range(NX):
        total = jnp.zeros((PIECE, 128), jnp.float32)
        for ts in range(N_TP):
            piece = recv_ref[xs * N_TP + ts].astype(jnp.float32)
            rows[xs * PIECE : (xs + 1) * PIECE, ts * 512 : (ts + 1) * 512] = piece[:, :512]
            total = total + piece[:, 512:]
        square = jnp.sum(total, axis=1, keepdims=True)
        scale = lax.rsqrt(square * (1.0 / D) + epsilon)
        here = slice(xs * PIECE, (xs + 1) * PIECE)
        rows[here, :] = rows[here, :] * scale
    out_ref[...] = rows[...].astype(jnp.bfloat16)


def norm_rows(received):
    return pl.pallas_call(
        norm_kernel,
        out_shape=jax.ShapeDtypeStruct((ROWS, D), jnp.bfloat16),
        scratch_shapes=[pltpu.VMEM((ROWS, D), jnp.float32)],
        name="norm_rows",
    )(received)


CHUNKS = 4
HALF = D // 2
DEEP = 512


def activate(rows, weights):
    both = jnp.dot(rows, weights, preferred_element_type=jnp.float32)
    gate = both[:, :128]
    return (gate / (1.0 + jnp.exp(-gate)) * both[:, 128:]).astype(jnp.bfloat16)


def starter(sems):
    numbers = iter(range(sems.shape[0]))

    def begin(source, target):
        copy = pltpu.make_async_copy(source, target, sems.at[next(numbers)])
        copy.start()
        return copy

    return begin


def near_kernel(all_ref, take_ref, *refs):
    in_refs = refs[:6]
    rows_ref, active_ref, gathered, in_buf, sems = refs[6:]
    begin = starter(sems)
    width = D // CHUNKS
    parts = [
        begin(all_ref.at[:, pl.ds(n * width, width)], gathered.at[n]) for n in range(CHUNKS)
    ]
    loads = [begin(in_refs[k], in_buf.at[k]) for k in range(6)]
    for n in range(CHUNKS):
        parts[n].wait()
        rows_ref[:, n * width : (n + 1) * width] = jnp.dot(
            take_ref[...], gathered[n], preferred_element_type=jnp.float32
        ).astype(jnp.bfloat16)
    for k in range(6):
        loads[k].wait()
        active_ref[k] = activate(rows_ref[...], in_buf[k])


def far_kernel(order_ref, rows_ref, active_ref, put_ref, low_ref, *refs):
    in_refs, down_refs = refs[:4], refs[4:14]
    out_ref, in_buf, down_buf, active, whole, parts, sems = refs[14:]
    begin = starter(sems)
    loads = [
        [
            begin(in_refs[2 * core], in_buf.at[core, pl.ds(0, HALF)]),
            begin(in_refs[2 * core + 1], in_buf.at[core, pl.ds(HALF, HALF)]),
        ]
        for core in range(NC)
    ]
    downs = []
    for core in range(NC):
        for k in range(NY):
            slot = core * NY + k
            group = [begin(low_ref.at[order_ref[slot]], down_buf.at[slot, pl.ds(0, DEEP)])]
            if k < 3:
                group.append(begin(down_refs[core * 5 + k], down_buf.at[slot, pl.ds(DEEP, DEEP)]))
            else:
                for i in range(2):
                    place = pl.ds(DEEP + i * DEEP // 2, DEEP // 2)
                    group.append(begin(down_refs[core * 5 + 3 + i], down_buf.at[slot, place]))
            downs.append(group)
    for core in range(NC):
        for k in range(3):
            active[order_ref[core * NY + k]] = active_ref[core * 3 + k]
        for copy in loads[core]:
            copy.wait()
        active[order_ref[core * NY + 3]] = activate(rows_ref[...], in_buf[core])
    for t in range(N_TP):
        whole[:, t * 128 : (t + 1) * 128] = active[t]
    outs = []
    for slot in range(N_TP):
        for copy in downs[slot]:
            copy.wait()
        part = jnp.dot(whole[...], down_buf[slot], preferred_element_type=jnp.float32)
        parts[slot] = jnp.dot(
            put_ref[...], part.astype(jnp.bfloat16), preferred_element_type=jnp.float32
        ).astype(jnp.bfloat16)
        lanes = pl.ds(pl.multiple_of(order_ref[slot] * 512, 512), 512)
        outs.append(begin(parts.at[slot], out_ref.at[:, lanes]))
    for copy in outs:
        copy.wait()


def run_experts(order, all_rows, take, put, near_in, far_in, low_down, high_down):
    far = pl.BlockSpec(memory_space=pltpu.HBM)
    local = pl.BlockSpec(memory_space=pltpu.VMEM)
    rows, active = pl.pallas_call(
        near_kernel,
        out_shape=(
            jax.ShapeDtypeStruct((OWN_ROWS, D), jnp.bfloat16),
            jax.ShapeDtypeStruct((6, OWN_ROWS, 128), jnp.bfloat16),
        ),
        in_specs=[far, local] + [far] * 6,
        out_specs=(local, local),
        scratch_shapes=[
            pltpu.VMEM((CHUNKS, ALL_ROWS, D // CHUNKS), jnp.bfloat16),
            pltpu.VMEM((6, D, 256), jnp.bfloat16),
            pltpu.SemaphoreType.DMA((CHUNKS + 6,)),
        ],
        compiler_params=pltpu.CompilerParams(vmem_limit_bytes=NEAR_VMEM),
        name="near_experts",
    )(all_rows, take, *near_in)
    return pl.pallas_call(
        far_kernel,
        out_shape=jax.ShapeDtypeStruct((ALL_ROWS, D), jnp.bfloat16),
        in_specs=[pl.BlockSpec(memory_space=pltpu.SMEM)] + [local] * 3 + [far] * 15,
        out_specs=far,
        scratch_shapes=[
            pltpu.VMEM((NC, D, 256), jnp.bfloat16),
            pltpu.VMEM((N_TP, 1024, 512), jnp.bfloat16),
            pltpu.VMEM((N_TP, OWN_ROWS, 128), jnp.bfloat16),
            pltpu.VMEM((OWN_ROWS, 1024), jnp.bfloat16),
            pltpu.VMEM((N_TP, ALL_ROWS, 512), jnp.bfloat16),
            pltpu.SemaphoreType.DMA((30,)),
        ],
        compiler_params=pltpu.CompilerParams(vmem_limit_bytes=FAR_VMEM),
        name="far_experts",
    )(order, rows, active, put, low_down, *far_in, *high_down)


NEAR_VMEM = 50 << 20
FAR_VMEM = 50 << 20


def by_y(value, step):
    return lax.ppermute(value, "y", [(i, (i + step) % NY) for i in range(NY)])


def other_core(value):
    return lax.ppermute(value, "c", [(0, 1), (1, 0)])


def both_cores(pieces):
    return pieces + [other_core(piece) for piece in pieces]


def far_halves(below, above):
    half = below.shape[0] // 2
    return both_cores([by_y(below[:half], 1), by_y(above[half:], -1)])


def three_parts(values):
    parts = []
    for _ in range(3):
        head = lax.reduce_precision(values, 8, 7)
        parts.append(head.astype(jnp.bfloat16))
        values = values - head
    return parts


def per_device(
    queries,
    fresh_kv,
    kv_pool,
    residual,
    norm_gain,
    gate_up,
    down_proj,
    prior_len,
    new_len,
    page_table,
    leaving,
    expert_ids,
    route_logits,
):
    my_z = lax.axis_index("z")
    my_group = lax.axis_index("x") * NZ + my_z
    leave_slot = leaving[my_group]
    handing = [(i, (i + 1) % N_REP) for i in range(N_REP)]

    in_own = gate_up[0]
    low_down = lax.all_gather(down_proj[0, :DEEP], TP)
    down_own = down_proj[0, DEEP:]
    mixed = jnp.concatenate(
        [queries.reshape(-1, N_TP, 512), fresh_kv.reshape(-1, N_TP, 256)], axis=2
    )
    heads = lax.all_to_all(mixed, TP, split_axis=1, concat_axis=0, tiled=True)[:, 0]
    query_heads, kv_rows = heads[:, :512], heads[:, 512:]
    resid_slots = residual.reshape(REQ, FRESH, -1)
    resid_came = lax.ppermute(
        lax.dynamic_index_in_dim(resid_slots, leave_slot, 0, keepdims=False), REP, handing
    )
    tables = page_table[0].reshape(REQ, PRIOR // PAGE)
    earlier = kv_pool[tables].reshape(REQ, PRIOR, -1)
    own_prior = lax.dynamic_slice_in_dim(prior_len, my_group * REQ, REQ, 0)
    own_new = lax.dynamic_slice_in_dim(new_len, my_group * REQ, REQ, 0)
    attention = attend_slots(
        query_heads.reshape(REQ, FRESH, -1),
        earlier,
        kv_rows.reshape(REQ, FRESH, -1),
        own_prior,
        own_new,
    )
    attention_came = lax.ppermute(
        lax.dynamic_index_in_dim(attention, leave_slot, 0, keepdims=False), REP, handing
    )
    is_new = (jnp.arange(REQ, dtype=jnp.int32) == leave_slot)[:, None, None]
    resid_new = jnp.where(is_new, resid_came[None], resid_slots).astype(jnp.float32)
    attention_new = jnp.where(is_new, attention_came[None], attention).astype(jnp.float32)
    token_count = REQ * FRESH
    hidden = (resid_new + attention_new).reshape(token_count, -1)

    struck = (
        expert_ids[:, :, None] == jnp.arange(EXPERTS, dtype=jnp.int32)[None, None, :]
    ).astype(jnp.bfloat16)
    loads = struck[:, 0] + struck[:, 1]
    earlier_rows = (
        jnp.arange(token_count, dtype=jnp.int32)[:, None]
        > jnp.arange(token_count, dtype=jnp.int32)[None, :]
    ).astype(jnp.bfloat16)
    ahead = jnp.dot(earlier_rows, loads, preferred_element_type=jnp.float32)
    place = jnp.sum(struck.astype(jnp.float32) * ahead[:, None, :], axis=2).astype(jnp.int32)
    target = (
        ((expert_ids // 2) * N_TP + place // SHARE) * PIECE + (expert_ids % 2) * SHARE + place % SHARE
    )
    slots = jnp.arange(EXPERTS * CAP, dtype=jnp.int32)
    placing = (
        (target[:, 0][None, :] == slots[:, None]) | (target[:, 1][None, :] == slots[:, None])
    ).astype(jnp.bfloat16)

    squares = three_parts(jnp.sum(hidden * hidden, axis=1))
    extra = jnp.stack(squares + [jnp.zeros_like(squares[0])], axis=1)
    extra = jnp.pad(extra, ((0, 0), (0, WIDE - 512 - 4)))
    payload = jnp.concatenate(
        [(hidden * norm_gain[None, :]).astype(jnp.bfloat16), extra], axis=1
    )
    packed = jnp.dot(placing, payload, preferred_element_type=jnp.float32).astype(jnp.bfloat16)
    received = lax.all_to_all(packed.reshape(NX * N_TP, PIECE, WIDE), SPREAD, 0, 0)
    normed = norm_rows(received.reshape(NX * N_TP, PIECE, WIDE))
    normed, in_own, low_down = lax.optimization_barrier((normed, in_own, low_down))
    all_rows = lax.all_gather(normed, "z", tiled=True)
    in_below, in_above, down_own = lax.optimization_barrier(
        (by_y(in_own, 1), by_y(in_own, -1), down_own)
    )
    far_in = far_halves(in_below, in_above)
    near_in = both_cores([in_own, in_below, in_above])
    down_below, down_above = by_y(down_own, 1), by_y(down_own, -1)
    near_down = both_cores([down_own, down_below, down_above])
    far_down = far_halves(down_below, down_above)
    high_down = near_down[:3] + far_down[:2] + near_down[3:] + far_down[2:]
    my_y, my_core = lax.axis_index("y"), lax.axis_index("c")
    piece = jnp.arange(N_TP, dtype=jnp.int32)
    step = piece % 4
    step = jnp.where(step == 1, NY - 1, jnp.where(step == 2, 1, jnp.where(step == 3, 2, 0)))
    order = (my_y + step) % NY * NC + (my_core + piece // 4) % NC

    index = jnp.arange(ALL_ROWS, dtype=jnp.int32)
    own = (index // SHARE) % 2 == my_z // 8
    compact = jnp.where(own, (index // PIECE) * SHARE + index % SHARE, -1)
    own_index = jnp.arange(OWN_ROWS, dtype=jnp.int32)
    take = (own_index[:, None] == compact[None, :]).astype(jnp.bfloat16)
    put = (compact[:, None] == own_index[None, :]).astype(jnp.bfloat16)
    partial_rows = run_experts(
        order, all_rows, take, put, near_in, far_in, low_down, high_down
    )
    summed = lax.psum_scatter(partial_rows, "z", scatter_dimension=0, tiled=True)
    back = summed.reshape(NX, PIECE, N_TP, 512).transpose(0, 2, 1, 3)
    returned = lax.all_to_all(back.reshape(NX * N_TP, PIECE, 512), SPREAD, 0, 0)
    returned = returned.reshape(EXPERTS * CAP, 512)
    shares = jax.nn.softmax(route_logits, axis=-1)
    first = (target[:, 0][:, None] == slots[None, :]).astype(jnp.bfloat16)
    second = (target[:, 1][:, None] == slots[None, :]).astype(jnp.bfloat16)
    moe_out = shares[:, 0:1] * jnp.dot(
        first, returned, preferred_element_type=jnp.float32
    ) + shares[:, 1:2] * jnp.dot(second, returned, preferred_element_type=jnp.float32)
    return (hidden + moe_out).astype(jnp.bfloat16)


def solution(mesh):
    inner = Mesh(mesh.devices.reshape(NX, NZ, NY, NC), ("x", "z", "y", "c"))
    every = ("x", "z", "y", "c")
    in_specs = (
        P(every, None),
        P(every, None),
        P(REP, None, TP),
        P(REP, TP),
        P(TP),
        P(REP, None, TP),
        P(REP, None, TP),
        P(),
        P(),
        P(REP, None),
        P(),
        P(REP, None),
        P(REP, None),
    )
    return jax.shard_map(
        per_device, mesh=inner, in_specs=in_specs, out_specs=P(REP, TP), check_vma=False
    )
```

```python
import functools

import jax
import jax.numpy as jnp
from jax import lax
from jax.experimental import pallas as pl
from jax.experimental.pallas import tpu as pltpu
from jax.sharding import Mesh
from jax.sharding import PartitionSpec as P

D = 4096
HD = 128
EXPERTS = 8
REQ = 4
FRESH = 32
PRIOR = 512
PAGE = 16
CAP = 40

NX, NZ, NY, NC = 4, 16, 4, 2
N_REP = NX * NZ
N_TP = NY * NC
REP = ("x", "z")
TP = ("y", "c")
SPREAD = ("x", "y", "c")
SHARE = CAP // N_TP
PIECE = 2 * SHARE
ROWS = NX * PIECE
ALL_ROWS = NZ * ROWS
OWN_ROWS = ALL_ROWS // 2
WIDE = 640

epsilon = 1e-05


def attend_slots(query_rows, earlier, newer, prior_count, new_count):
    requests, fresh_len, q_width = query_rows.shape
    group_size = q_width // HD
    keys_all = jnp.concatenate([earlier, newer], axis=1)
    span_len = keys_all.shape[1]
    prior_span = earlier.shape[1]
    key_part = keys_all[:, :, :HD]
    value_part = keys_all[:, :, HD:]
    grouped = query_rows.reshape(requests, fresh_len, group_size, HD)
    scores = jnp.einsum(
        "rcjd,rkd->rjck", grouped, key_part, preferred_element_type=jnp.float32
    ) * HD ** (-0.5)
    key_pos = jnp.arange(span_len, dtype=jnp.int32)
    key_offset = key_pos - prior_span
    query_pos = jnp.arange(fresh_len, dtype=jnp.int32)
    visible = jnp.where(
        key_pos[None, None, :] < prior_span,
        key_pos[None, None, :] < prior_count[:, None, None],
        (key_offset[None, None, :] <= query_pos[None, :, None])
        & (key_offset[None, None, :] < new_count[:, None, None]),
    )
    visible = visible[:, None]
    masked = jnp.where(visible, scores, -1e30)
    highest = jnp.max(masked, axis=-1, keepdims=True)
    expo = jnp.where(visible, jnp.exp(masked - highest), 0.0)
    totals = jnp.sum(expo, axis=-1, keepdims=True)
    weights = (expo / totals).astype(jnp.bfloat16)
    mixed = jnp.einsum("rjck,rkd->rcjd", weights, value_part, preferred_element_type=jnp.float32)
    mixed = mixed.reshape(requests, fresh_len, q_width)
    return jnp.where(query_pos[None, :, None] < new_count[:, None, None], mixed, 0.0).astype(
        jnp.bfloat16
    )


def norm_kernel(recv_ref, out_ref, rows):
    for xs in range(NX):
        total = jnp.zeros((PIECE, 128), jnp.float32)
        for ts in range(N_TP):
            piece = recv_ref[xs * N_TP + ts].astype(jnp.float32)
            rows[xs * PIECE : (xs + 1) * PIECE, ts * 512 : (ts + 1) * 512] = piece[:, :512]
            total = total + piece[:, 512:]
        square = jnp.sum(total, axis=1, keepdims=True)
        scale = lax.rsqrt(square * (1.0 / D) + epsilon)
        here = slice(xs * PIECE, (xs + 1) * PIECE)
        rows[here, :] = rows[here, :] * scale
    out_ref[...] = rows[...].astype(jnp.bfloat16)


def norm_rows(received):
    return pl.pallas_call(
        norm_kernel,
        out_shape=jax.ShapeDtypeStruct((ROWS, D), jnp.bfloat16),
        scratch_shapes=[pltpu.VMEM((ROWS, D), jnp.float32)],
        name="norm_rows",
    )(received)


CHUNKS = 4
HALF = D // 2


def expert_kernel(order_ref, all_ref, take_ref, put_ref, *refs):
    in_refs, down_refs = refs[:10], refs[10:12]
    out_ref, gathered, rows, in_buf, down_buf, active, whole, sems = refs[12:]
    width = D // CHUNKS
    numbers = iter(range(sems.shape[0]))

    def begin(source, target):
        copy = pltpu.make_async_copy(source, target, sems.at[next(numbers)])
        copy.start()
        return copy

    parts = [
        begin(all_ref.at[:, pl.ds(n * width, width)], gathered.at[n]) for n in range(CHUNKS)
    ]
    loads = [None] * N_TP
    for core in range(NC):
        for k in range(3):
            slot = core * NY + k
            loads[slot] = [begin(in_refs[core * 5 + k], in_buf.at[slot])]
    for core in range(NC):
        chunk = in_buf.at[core * NY + 3]
        loads[core * NY + 3] = [
            begin(in_refs[core * 5 + 3 + i], chunk.at[pl.ds(i * HALF, HALF)]) for i in range(2)
        ]
    downs = [
        begin(down_refs[core].at[k], down_buf.at[core * NY + k])
        for core in range(NC)
        for k in range(NY)
    ]
    for n in range(CHUNKS):
        parts[n].wait()
        rows[:, n * width : (n + 1) * width] = jnp.dot(
            take_ref[...], gathered[n], preferred_element_type=jnp.float32
        ).astype(jnp.bfloat16)
    for slot in (0, 1, 2, 4, 5, 6, 3, 7):
        for copy in loads[slot]:
            copy.wait()
        both = jnp.dot(rows[...], in_buf[slot], preferred_element_type=jnp.float32)
        gate = both[:, :128]
        active[order_ref[slot]] = (gate / (1.0 + jnp.exp(-gate)) * both[:, 128:]).astype(
            jnp.bfloat16
        )
    for t in range(N_TP):
        whole[:, t * 128 : (t + 1) * 128] = active[t]
    outs = []
    for slot in range(N_TP):
        downs[slot].wait()
        part = jnp.dot(whole[...], down_buf[slot], preferred_element_type=jnp.float32)
        place = gathered.at[slot // 2, :, pl.ds(slot % 2 * 512, 512)]
        place[...] = jnp.dot(
            put_ref[...], part.astype(jnp.bfloat16), preferred_element_type=jnp.float32
        ).astype(jnp.bfloat16)
        lanes = pl.ds(pl.multiple_of(order_ref[N_TP + slot] * 512, 512), 512)
        outs.append(begin(place, out_ref.at[:, lanes]))
    for copy in outs:
        copy.wait()


def run_experts(order, all_rows, take, put, weights_in, weights_down):
    far = pl.BlockSpec(memory_space=pltpu.HBM)
    local = pl.BlockSpec(memory_space=pltpu.VMEM)
    return pl.pallas_call(
        expert_kernel,
        out_shape=jax.ShapeDtypeStruct((ALL_ROWS, D), jnp.bfloat16),
        in_specs=[pl.BlockSpec(memory_space=pltpu.SMEM), far, local, local] + [far] * 12,
        out_specs=far,
        scratch_shapes=[
            pltpu.VMEM((CHUNKS, ALL_ROWS, D // CHUNKS), jnp.bfloat16),
            pltpu.VMEM((OWN_ROWS, D), jnp.bfloat16),
            pltpu.VMEM((N_TP, D, 256), jnp.bfloat16),
            pltpu.VMEM((N_TP, 1024, 512), jnp.bfloat16),
            pltpu.VMEM((N_TP, OWN_ROWS, 128), jnp.bfloat16),
            pltpu.VMEM((OWN_ROWS, 1024), jnp.bfloat16),
            pltpu.SemaphoreType.DMA((CHUNKS + 10 + 2 * N_TP,)),
        ],
        compiler_params=pltpu.CompilerParams(vmem_limit_bytes=50 << 20),
        name="experts",
    )(order, all_rows, take, put, *weights_in, *weights_down)


def by_y(value, step):
    return lax.ppermute(value, "y", [(i, (i + step) % NY) for i in range(NY)])


def other_core(value):
    return lax.ppermute(value, "c", [(0, 1), (1, 0)])


def both_cores(pieces):
    return pieces + [other_core(piece) for piece in pieces]


def three_parts(values):
    parts = []
    for _ in range(3):
        head = lax.reduce_precision(values, 8, 7)
        parts.append(head.astype(jnp.bfloat16))
        values = values - head
    return parts


def per_device(
    queries,
    fresh_kv,
    kv_pool,
    residual,
    norm_gain,
    gate_up,
    down_proj,
    prior_len,
    new_len,
    page_table,
    leaving,
    expert_ids,
    route_logits,
):
    my_z = lax.axis_index("z")
    my_group = lax.axis_index("x") * NZ + my_z
    leave_slot = leaving[my_group]
    handing = [(i, (i + 1) % N_REP) for i in range(N_REP)]

    in_own = gate_up[0]
    down_mine = lax.all_gather(down_proj[0], "y")
    mixed = jnp.concatenate(
        [queries.reshape(-1, N_TP, 512), fresh_kv.reshape(-1, N_TP, 256)], axis=2
    )
    heads = lax.all_to_all(mixed, TP, split_axis=1, concat_axis=0, tiled=True)[:, 0]
    query_heads, kv_rows = heads[:, :512], heads[:, 512:]
    resid_slots = residual.reshape(REQ, FRESH, -1)
    resid_came = lax.ppermute(
        lax.dynamic_index_in_dim(resid_slots, leave_slot, 0, keepdims=False), REP, handing
    )
    tables = page_table[0].reshape(REQ, PRIOR // PAGE)
    earlier = kv_pool[tables].reshape(REQ, PRIOR, -1)
    own_prior = lax.dynamic_slice_in_dim(prior_len, my_group * REQ, REQ, 0)
    own_new = lax.dynamic_slice_in_dim(new_len, my_group * REQ, REQ, 0)
    attention = attend_slots(
        query_heads.reshape(REQ, FRESH, -1),
        earlier,
        kv_rows.reshape(REQ, FRESH, -1),
        own_prior,
        own_new,
    )
    attention_came = lax.ppermute(
        lax.dynamic_index_in_dim(attention, leave_slot, 0, keepdims=False), REP, handing
    )
    is_new = (jnp.arange(REQ, dtype=jnp.int32) == leave_slot)[:, None, None]
    resid_new = jnp.where(is_new, resid_came[None], resid_slots).astype(jnp.float32)
    attention_new = jnp.where(is_new, attention_came[None], attention).astype(jnp.float32)
    token_count = REQ * FRESH
    hidden = (resid_new + attention_new).reshape(token_count, -1)

    struck = (
        expert_ids[:, :, None] == jnp.arange(EXPERTS, dtype=jnp.int32)[None, None, :]
    ).astype(jnp.bfloat16)
    loads = struck[:, 0] + struck[:, 1]
    earlier_rows = (
        jnp.arange(token_count, dtype=jnp.int32)[:, None]
        > jnp.arange(token_count, dtype=jnp.int32)[None, :]
    ).astype(jnp.bfloat16)
    ahead = jnp.dot(earlier_rows, loads, preferred_element_type=jnp.float32)
    place = jnp.sum(struck.astype(jnp.float32) * ahead[:, None, :], axis=2).astype(jnp.int32)
    target = (
        ((expert_ids // 2) * N_TP + place // SHARE) * PIECE + (expert_ids % 2) * SHARE + place % SHARE
    )
    slots = jnp.arange(EXPERTS * CAP, dtype=jnp.int32)
    placing = (
        (target[:, 0][None, :] == slots[:, None]) | (target[:, 1][None, :] == slots[:, None])
    ).astype(jnp.bfloat16)

    squares = three_parts(jnp.sum(hidden * hidden, axis=1))
    extra = jnp.stack(squares + [jnp.zeros_like(squares[0])], axis=1)
    extra = jnp.pad(extra, ((0, 0), (0, WIDE - 512 - 4)))
    payload = jnp.concatenate(
        [(hidden * norm_gain[None, :]).astype(jnp.bfloat16), extra], axis=1
    )
    packed = jnp.dot(placing, payload, preferred_element_type=jnp.float32).astype(jnp.bfloat16)
    received = lax.all_to_all(packed.reshape(NX * N_TP, PIECE, WIDE), SPREAD, 0, 0)
    received, in_own = lax.optimization_barrier((received, in_own))
    in_below, in_above = by_y(in_own, 1), by_y(in_own, -1)
    normed = norm_rows(received.reshape(NX * N_TP, PIECE, WIDE))
    all_rows = lax.all_gather(normed, "z", tiled=True)
    in_below, in_above, in_own, down_mine = lax.optimization_barrier(
        (in_below, in_above, in_own, down_mine)
    )
    weights_down = both_cores([down_mine])
    far_in = [by_y(in_below[:HALF], 1), by_y(in_above[HALF:], -1)]
    weights_in = both_cores([in_own, in_below, in_above] + far_in)
    my_y, my_core = lax.axis_index("y"), lax.axis_index("c")
    piece = jnp.arange(2 * N_TP, dtype=jnp.int32)
    step = piece % NY
    step = jnp.where(step == 1, NY - 1, jnp.where(step == 2, 1, jnp.where(step == 3, 2, 0)))
    place_y = jnp.where(piece < N_TP, (my_y + step) % NY, piece % NY)
    order = place_y * NC + (my_core + piece // NY) % NC

    index = jnp.arange(ALL_ROWS, dtype=jnp.int32)
    own = (index // SHARE) % 2 == my_z // 8
    compact = jnp.where(own, (index // PIECE) * SHARE + index % SHARE, -1)
    own_index = jnp.arange(OWN_ROWS, dtype=jnp.int32)
    take = (own_index[:, None] == compact[None, :]).astype(jnp.bfloat16)
    put = (compact[:, None] == own_index[None, :]).astype(jnp.bfloat16)
    partial_rows = run_experts(order, all_rows, take, put, weights_in, weights_down)
    summed = lax.psum_scatter(partial_rows, "z", scatter_dimension=0, tiled=True)
    back = summed.reshape(NX, PIECE, N_TP, 512).transpose(0, 2, 1, 3)
    returned = lax.all_to_all(back.reshape(NX * N_TP, PIECE, 512), SPREAD, 0, 0)
    returned = returned.reshape(EXPERTS * CAP, 512)
    shares = jax.nn.softmax(route_logits, axis=-1)
    first = (target[:, 0][:, None] == slots[None, :]).astype(jnp.bfloat16)
    second = (target[:, 1][:, None] == slots[None, :]).astype(jnp.bfloat16)
    moe_out = shares[:, 0:1] * jnp.dot(
        first, returned, preferred_element_type=jnp.float32
    ) + shares[:, 1:2] * jnp.dot(second, returned, preferred_element_type=jnp.float32)
    return (hidden + moe_out).astype(jnp.bfloat16)


def solution(mesh):
    inner = Mesh(mesh.devices.reshape(NX, NZ, NY, NC), ("x", "z", "y", "c"))
    every = ("x", "z", "y", "c")
    in_specs = (
        P(every, None),
        P(every, None),
        P(REP, None, TP),
        P(REP, TP),
        P(TP),
        P(REP, None, TP),
        P(REP, None, TP),
        P(),
        P(),
        P(REP, None),
        P(),
        P(REP, None),
        P(REP, None),
    )
    return jax.shard_map(
        per_device, mesh=inner, in_specs=in_specs, out_specs=P(REP, TP), check_vma=False
    )
```

```python
import functools

import jax
import jax.numpy as jnp
from jax import lax
from jax.experimental import pallas as pl
from jax.experimental.pallas import tpu as pltpu
from jax.sharding import Mesh
from jax.sharding import PartitionSpec as P

D = 4096
HD = 128
EXPERTS = 8
REQ = 4
FRESH = 32
PRIOR = 512
PAGE = 16
CAP = 40

NX, NZ, NY, NC = 4, 16, 4, 2
N_REP = NX * NZ
N_TP = NY * NC
REP = ("x", "z")
TP = ("y", "c")
SPREAD = ("x", "y", "c")
SHARE = CAP // N_TP
PIECE = 2 * SHARE
ROWS = NX * PIECE
ALL_ROWS = NZ * ROWS
OWN_ROWS = ALL_ROWS // 2
WIDE = 640

epsilon = 1e-05


def attend_slots(query_rows, earlier, newer, prior_count, new_count):
    requests, fresh_len, q_width = query_rows.shape
    group_size = q_width // HD
    keys_all = jnp.concatenate([earlier, newer], axis=1)
    span_len = keys_all.shape[1]
    prior_span = earlier.shape[1]
    key_part = keys_all[:, :, :HD]
    value_part = keys_all[:, :, HD:]
    grouped = query_rows.reshape(requests, fresh_len, group_size, HD)
    scores = jnp.einsum(
        "rcjd,rkd->rjck", grouped, key_part, preferred_element_type=jnp.float32
    ) * HD ** (-0.5)
    key_pos = jnp.arange(span_len, dtype=jnp.int32)
    key_offset = key_pos - prior_span
    query_pos = jnp.arange(fresh_len, dtype=jnp.int32)
    visible = jnp.where(
        key_pos[None, None, :] < prior_span,
        key_pos[None, None, :] < prior_count[:, None, None],
        (key_offset[None, None, :] <= query_pos[None, :, None])
        & (key_offset[None, None, :] < new_count[:, None, None]),
    )
    visible = visible[:, None]
    masked = jnp.where(visible, scores, -1e30)
    highest = jnp.max(masked, axis=-1, keepdims=True)
    expo = jnp.where(visible, jnp.exp(masked - highest), 0.0)
    totals = jnp.sum(expo, axis=-1, keepdims=True)
    weights = (expo / totals).astype(jnp.bfloat16)
    mixed = jnp.einsum("rjck,rkd->rcjd", weights, value_part, preferred_element_type=jnp.float32)
    mixed = mixed.reshape(requests, fresh_len, q_width)
    return jnp.where(query_pos[None, :, None] < new_count[:, None, None], mixed, 0.0).astype(
        jnp.bfloat16
    )


def norm_kernel(recv_ref, out_ref, rows):
    for xs in range(NX):
        total = jnp.zeros((PIECE, 128), jnp.float32)
        for ts in range(N_TP):
            piece = recv_ref[xs * N_TP + ts].astype(jnp.float32)
            rows[xs * PIECE : (xs + 1) * PIECE, ts * 512 : (ts + 1) * 512] = piece[:, :512]
            total = total + piece[:, 512:]
        square = jnp.sum(total, axis=1, keepdims=True)
        scale = lax.rsqrt(square * (1.0 / D) + epsilon)
        here = slice(xs * PIECE, (xs + 1) * PIECE)
        rows[here, :] = rows[here, :] * scale
    out_ref[...] = rows[...].astype(jnp.bfloat16)


def norm_rows(received):
    return pl.pallas_call(
        norm_kernel,
        out_shape=jax.ShapeDtypeStruct((ROWS, D), jnp.bfloat16),
        scratch_shapes=[pltpu.VMEM((ROWS, D), jnp.float32)],
        name="norm_rows",
    )(received)


CHUNKS = 4
HALF = D // 2
DEEP = 512


def expert_kernel(order_ref, all_ref, take_ref, put_ref, *refs):
    in_refs, low_ref, high_refs = refs[:10], refs[10], refs[11:21]
    out_ref, gathered, rows, in_buf, down_buf, active, whole, sems = refs[21:]
    width = D // CHUNKS
    numbers = iter(range(sems.shape[0]))

    def begin(source, target):
        copy = pltpu.make_async_copy(source, target, sems.at[next(numbers)])
        copy.start()
        return copy

    parts = [
        begin(all_ref.at[:, pl.ds(n * width, width)], gathered.at[n]) for n in range(CHUNKS)
    ]
    loads = [None] * N_TP
    for core in range(NC):
        for k in range(3):
            slot = core * NY + k
            loads[slot] = [begin(in_refs[core * 5 + k], in_buf.at[slot])]
    for core in range(NC):
        chunk = in_buf.at[core * NY + 3]
        loads[core * NY + 3] = [
            begin(in_refs[core * 5 + 3 + i], chunk.at[pl.ds(i * HALF, HALF)]) for i in range(2)
        ]
    downs = []
    for core in range(NC):
        for k in range(NY):
            slot = core * NY + k
            group = [begin(low_ref.at[order_ref[slot]], down_buf.at[slot, pl.ds(0, DEEP)])]
            if k < 3:
                group.append(begin(high_refs[core * 5 + k], down_buf.at[slot, pl.ds(DEEP, DEEP)]))
            else:
                for i in range(2):
                    place = pl.ds(DEEP + i * DEEP // 2, DEEP // 2)
                    group.append(begin(high_refs[core * 5 + 3 + i], down_buf.at[slot, place]))
            downs.append(group)
    for n in range(CHUNKS):
        parts[n].wait()
        rows[:, n * width : (n + 1) * width] = jnp.dot(
            take_ref[...], gathered[n], preferred_element_type=jnp.float32
        ).astype(jnp.bfloat16)
    for slot in (0, 1, 2, 4, 5, 6, 3, 7):
        for copy in loads[slot]:
            copy.wait()
        both = jnp.dot(rows[...], in_buf[slot], preferred_element_type=jnp.float32)
        gate = both[:, :128]
        active[order_ref[slot]] = (gate / (1.0 + jnp.exp(-gate)) * both[:, 128:]).astype(
            jnp.bfloat16
        )
    for t in range(N_TP):
        whole[:, t * 128 : (t + 1) * 128] = active[t]
    outs = []
    for slot in range(N_TP):
        for copy in downs[slot]:
            copy.wait()
        part = jnp.dot(whole[...], down_buf[slot], preferred_element_type=jnp.float32)
        place = gathered.at[slot // 2, :, pl.ds(slot % 2 * 512, 512)]
        place[...] = jnp.dot(
            put_ref[...], part.astype(jnp.bfloat16), preferred_element_type=jnp.float32
        ).astype(jnp.bfloat16)
        lanes = pl.ds(pl.multiple_of(order_ref[slot] * 512, 512), 512)
        outs.append(begin(place, out_ref.at[:, lanes]))
    for copy in outs:
        copy.wait()


def run_experts(order, all_rows, take, put, weights_in, low_down, high_down):
    far = pl.BlockSpec(memory_space=pltpu.HBM)
    local = pl.BlockSpec(memory_space=pltpu.VMEM)
    return pl.pallas_call(
        expert_kernel,
        out_shape=jax.ShapeDtypeStruct((ALL_ROWS, D), jnp.bfloat16),
        in_specs=[pl.BlockSpec(memory_space=pltpu.SMEM), far, local, local] + [far] * 21,
        out_specs=far,
        scratch_shapes=[
            pltpu.VMEM((CHUNKS, ALL_ROWS, D // CHUNKS), jnp.bfloat16),
            pltpu.VMEM((OWN_ROWS, D), jnp.bfloat16),
            pltpu.VMEM((N_TP, D, 256), jnp.bfloat16),
            pltpu.VMEM((N_TP, 1024, 512), jnp.bfloat16),
            pltpu.VMEM((N_TP, OWN_ROWS, 128), jnp.bfloat16),
            pltpu.VMEM((OWN_ROWS, 1024), jnp.bfloat16),
            pltpu.SemaphoreType.DMA((CHUNKS + 10 + 18 + N_TP,)),
        ],
        compiler_params=pltpu.CompilerParams(vmem_limit_bytes=50 << 20),
        name="experts",
    )(order, all_rows, take, put, *weights_in, low_down, *high_down)


def by_y(value, step):
    return lax.ppermute(value, "y", [(i, (i + step) % NY) for i in range(NY)])


def other_core(value):
    return lax.ppermute(value, "c", [(0, 1), (1, 0)])


def three_parts(values):
    parts = []
    for _ in range(3):
        head = lax.reduce_precision(values, 8, 7)
        parts.append(head.astype(jnp.bfloat16))
        values = values - head
    return parts


def per_device(
    queries,
    fresh_kv,
    kv_pool,
    residual,
    norm_gain,
    gate_up,
    down_proj,
    prior_len,
    new_len,
    page_table,
    leaving,
    expert_ids,
    route_logits,
):
    my_z = lax.axis_index("z")
    my_group = lax.axis_index("x") * NZ + my_z
    leave_slot = leaving[my_group]
    handing = [(i, (i + 1) % N_REP) for i in range(N_REP)]

    in_own = gate_up[0]
    low_down = lax.all_gather(down_proj[0, :DEEP], TP)
    down_own = down_proj[0, DEEP:]
    mixed = jnp.concatenate(
        [queries.reshape(-1, N_TP, 512), fresh_kv.reshape(-1, N_TP, 256)], axis=2
    )
    heads = lax.all_to_all(mixed, TP, split_axis=1, concat_axis=0, tiled=True)[:, 0]
    heads, down_own = lax.optimization_barrier((heads, down_own))
    down_below, down_above = by_y(down_own, 1), by_y(down_own, -1)
    query_heads, kv_rows = heads[:, :512], heads[:, 512:]
    resid_slots = residual.reshape(REQ, FRESH, -1)
    resid_came = lax.ppermute(
        lax.dynamic_index_in_dim(resid_slots, leave_slot, 0, keepdims=False), REP, handing
    )
    tables = page_table[0].reshape(REQ, PRIOR // PAGE)
    earlier = kv_pool[tables].reshape(REQ, PRIOR, -1)
    own_prior = lax.dynamic_slice_in_dim(prior_len, my_group * REQ, REQ, 0)
    own_new = lax.dynamic_slice_in_dim(new_len, my_group * REQ, REQ, 0)
    attention = attend_slots(
        query_heads.reshape(REQ, FRESH, -1),
        earlier,
        kv_rows.reshape(REQ, FRESH, -1),
        own_prior,
        own_new,
    )
    attention_came = lax.ppermute(
        lax.dynamic_index_in_dim(attention, leave_slot, 0, keepdims=False), REP, handing
    )
    is_new = (jnp.arange(REQ, dtype=jnp.int32) == leave_slot)[:, None, None]
    resid_new = jnp.where(is_new, resid_came[None], resid_slots).astype(jnp.float32)
    attention_new = jnp.where(is_new, attention_came[None], attention).astype(jnp.float32)
    token_count = REQ * FRESH
    hidden = (resid_new + attention_new).reshape(token_count, -1)

    struck = (
        expert_ids[:, :, None] == jnp.arange(EXPERTS, dtype=jnp.int32)[None, None, :]
    ).astype(jnp.bfloat16)
    loads = struck[:, 0] + struck[:, 1]
    earlier_rows = (
        jnp.arange(token_count, dtype=jnp.int32)[:, None]
        > jnp.arange(token_count, dtype=jnp.int32)[None, :]
    ).astype(jnp.bfloat16)
    ahead = jnp.dot(earlier_rows, loads, preferred_element_type=jnp.float32)
    place = jnp.sum(struck.astype(jnp.float32) * ahead[:, None, :], axis=2).astype(jnp.int32)
    target = (
        ((expert_ids // 2) * N_TP + place // SHARE) * PIECE + (expert_ids % 2) * SHARE + place % SHARE
    )
    slots = jnp.arange(EXPERTS * CAP, dtype=jnp.int32)
    placing = (
        (target[:, 0][None, :] == slots[:, None]) | (target[:, 1][None, :] == slots[:, None])
    ).astype(jnp.bfloat16)

    squares = three_parts(jnp.sum(hidden * hidden, axis=1))
    extra = jnp.stack(squares + [jnp.zeros_like(squares[0])], axis=1)
    extra = jnp.pad(extra, ((0, 0), (0, WIDE - 512 - 4)))
    payload = jnp.concatenate(
        [(hidden * norm_gain[None, :]).astype(jnp.bfloat16), extra], axis=1
    )
    packed = jnp.dot(placing, payload, preferred_element_type=jnp.float32).astype(jnp.bfloat16)
    received = lax.all_to_all(packed.reshape(NX * N_TP, PIECE, WIDE), SPREAD, 0, 0)
    received, in_own, down_own, down_below, down_above = lax.optimization_barrier(
        (received, in_own, down_own, down_below, down_above)
    )
    in_below, in_above = by_y(in_own, 1), by_y(in_own, -1)
    normed = norm_rows(received.reshape(NX * N_TP, PIECE, WIDE))
    all_rows = lax.all_gather(normed, "z", tiled=True)
    far_down = [by_y(down_below[: DEEP // 2], 1), by_y(down_above[DEEP // 2 :], -1)]
    other_own = other_core(in_own)
    other_down = [other_core(piece) for piece in (down_own, down_below, down_above)]
    in_below, in_above, far_down, low_down = lax.optimization_barrier(
        (in_below, in_above, far_down, low_down)
    )
    far_in = [by_y(in_below[:HALF], 1), by_y(in_above[HALF:], -1)]
    other_in = [other_own, other_core(in_below), other_core(in_above)]
    weights_in = [in_own, in_below, in_above] + far_in + other_in
    weights_in += [other_core(piece) for piece in far_in]
    high_down = [down_own, down_below, down_above] + far_down + other_down
    high_down += [other_core(piece) for piece in far_down]
    my_y, my_core = lax.axis_index("y"), lax.axis_index("c")
    piece = jnp.arange(N_TP, dtype=jnp.int32)
    step = piece % NY
    step = jnp.where(step == 1, NY - 1, jnp.where(step == 2, 1, jnp.where(step == 3, 2, 0)))
    order = (my_y + step) % NY * NC + (my_core + piece // NY) % NC

    index = jnp.arange(ALL_ROWS, dtype=jnp.int32)
    own = (index // SHARE) % 2 == my_z // 8
    compact = jnp.where(own, (index // PIECE) * SHARE + index % SHARE, -1)
    own_index = jnp.arange(OWN_ROWS, dtype=jnp.int32)
    take = (own_index[:, None] == compact[None, :]).astype(jnp.bfloat16)
    put = (compact[:, None] == own_index[None, :]).astype(jnp.bfloat16)
    partial_rows = run_experts(
        order, all_rows, take, put, weights_in, low_down, high_down
    )
    summed = lax.psum_scatter(partial_rows, "z", scatter_dimension=0, tiled=True)
    back = summed.reshape(NX, PIECE, N_TP, 512).transpose(0, 2, 1, 3)
    returned = lax.all_to_all(back.reshape(NX * N_TP, PIECE, 512), SPREAD, 0, 0)
    returned = returned.reshape(EXPERTS * CAP, 512)
    shares = jax.nn.softmax(route_logits, axis=-1)
    first = (target[:, 0][:, None] == slots[None, :]).astype(jnp.bfloat16)
    second = (target[:, 1][:, None] == slots[None, :]).astype(jnp.bfloat16)
    moe_out = shares[:, 0:1] * jnp.dot(
        first, returned, preferred_element_type=jnp.float32
    ) + shares[:, 1:2] * jnp.dot(second, returned, preferred_element_type=jnp.float32)
    return (hidden + moe_out).astype(jnp.bfloat16)


def solution(mesh):
    inner = Mesh(mesh.devices.reshape(NX, NZ, NY, NC), ("x", "z", "y", "c"))
    every = ("x", "z", "y", "c")
    in_specs = (
        P(every, None),
        P(every, None),
        P(REP, None, TP),
        P(REP, TP),
        P(TP),
        P(REP, None, TP),
        P(REP, None, TP),
        P(),
        P(),
        P(REP, None),
        P(),
        P(REP, None),
        P(REP, None),
    )
    return jax.shard_map(
        per_device, mesh=inner, in_specs=in_specs, out_specs=P(REP, TP), check_vma=False
    )
```

```python
import functools

import jax
import jax.numpy as jnp
from jax import lax
from jax.experimental import pallas as pl
from jax.experimental.pallas import tpu as pltpu
from jax.sharding import Mesh
from jax.sharding import PartitionSpec as P

D = 4096
HD = 128
EXPERTS = 8
REQ = 4
FRESH = 32
PRIOR = 512
PAGE = 16
CAP = 40

NX, NZ, NY, NC = 4, 16, 4, 2
N_REP = NX * NZ
N_TP = NY * NC
REP = ("x", "z")
TP = ("y", "c")
SPREAD = ("x", "y", "c")
SHARE = CAP // N_TP
PIECE = 2 * SHARE
ROWS = NX * PIECE
ALL_ROWS = NZ * ROWS
OWN_ROWS = ALL_ROWS // 2
WIDE = 640

epsilon = 1e-05


def attend_slots(query_rows, earlier, newer, prior_count, new_count):
    requests, fresh_len, q_width = query_rows.shape
    group_size = q_width // HD
    keys_all = jnp.concatenate([earlier, newer], axis=1)
    span_len = keys_all.shape[1]
    prior_span = earlier.shape[1]
    key_part = keys_all[:, :, :HD]
    value_part = keys_all[:, :, HD:]
    grouped = query_rows.reshape(requests, fresh_len, group_size, HD)
    scores = jnp.einsum(
        "rcjd,rkd->rjck", grouped, key_part, preferred_element_type=jnp.float32
    ) * HD ** (-0.5)
    key_pos = jnp.arange(span_len, dtype=jnp.int32)
    key_offset = key_pos - prior_span
    query_pos = jnp.arange(fresh_len, dtype=jnp.int32)
    visible = jnp.where(
        key_pos[None, None, :] < prior_span,
        key_pos[None, None, :] < prior_count[:, None, None],
        (key_offset[None, None, :] <= query_pos[None, :, None])
        & (key_offset[None, None, :] < new_count[:, None, None]),
    )
    visible = visible[:, None]
    masked = jnp.where(visible, scores, -1e30)
    highest = jnp.max(masked, axis=-1, keepdims=True)
    expo = jnp.where(visible, jnp.exp(masked - highest), 0.0)
    totals = jnp.sum(expo, axis=-1, keepdims=True)
    weights = (expo / totals).astype(jnp.bfloat16)
    mixed = jnp.einsum("rjck,rkd->rcjd", weights, value_part, preferred_element_type=jnp.float32)
    mixed = mixed.reshape(requests, fresh_len, q_width)
    return jnp.where(query_pos[None, :, None] < new_count[:, None, None], mixed, 0.0).astype(
        jnp.bfloat16
    )


def norm_kernel(recv_ref, out_ref, rows):
    for xs in range(NX):
        total = jnp.zeros((PIECE, 128), jnp.float32)
        for ts in range(N_TP):
            piece = recv_ref[xs * N_TP + ts].astype(jnp.float32)
            rows[xs * PIECE : (xs + 1) * PIECE, ts * 512 : (ts + 1) * 512] = piece[:, :512]
            total = total + piece[:, 512:]
        square = jnp.sum(total, axis=1, keepdims=True)
        scale = lax.rsqrt(square * (1.0 / D) + epsilon)
        here = slice(xs * PIECE, (xs + 1) * PIECE)
        rows[here, :] = rows[here, :] * scale
    out_ref[...] = rows[...].astype(jnp.bfloat16)


def norm_rows(received):
    return pl.pallas_call(
        norm_kernel,
        out_shape=jax.ShapeDtypeStruct((ROWS, D), jnp.bfloat16),
        scratch_shapes=[pltpu.VMEM((ROWS, D), jnp.float32)],
        name="norm_rows",
    )(received)


CHUNKS = 4


def expert_kernel(order_ref, all_ref, take_ref, put_ref, *refs):
    in_refs, down_hbm = refs[:14], refs[14]
    out_ref, gathered, rows, in_buf, down_buf, active, whole, sems = refs[15:]
    width = D // CHUNKS
    half = D // 2
    count = iter(range(30))

    def begin(source, target):
        copy = pltpu.make_async_copy(source, target, sems.at[next(count)])
        copy.start()
        return copy

    parts = [
        begin(all_ref.at[:, pl.ds(n * width, width)], gathered.at[n]) for n in range(CHUNKS)
    ]

    def load(slot):
        chunk, first = in_buf.at[slot], slot // NY * 7 + 2 * (slot % NY)
        if slot % NY == 0:
            return [begin(in_refs[first], chunk)]
        return [
            begin(in_refs[first - 1], chunk.at[pl.ds(0, half)]),
            begin(in_refs[first], chunk.at[pl.ds(half, half)]),
        ]

    loads = [load(0)]
    for n in range(CHUNKS):
        parts[n].wait()
        rows[:, n * width : (n + 1) * width] = jnp.dot(
            take_ref[...], gathered[n], preferred_element_type=jnp.float32
        ).astype(jnp.bfloat16)
        if n == 1:
            loads.append(load(1))
    loads.append(load(2))
    downs = []
    for k in range(N_TP):
        if k + 3 < N_TP:
            loads.append(load(k + 3))
        downs.append(begin(down_hbm.at[k], down_buf.at[k]))
        for copy in loads[k]:
            copy.wait()
        both = jnp.dot(rows[...], in_buf[k], preferred_element_type=jnp.float32)
        gate = both[:, :128]
        active[order_ref[k]] = (gate / (1.0 + jnp.exp(-gate)) * both[:, 128:]).astype(jnp.bfloat16)
    for t in range(N_TP):
        whole[:, t * 128 : (t + 1) * 128] = active[t]
    outs = []
    for t in range(N_TP):
        downs[t].wait()
        part = jnp.dot(whole[...], down_buf[t], preferred_element_type=jnp.float32)
        n, lane = t // 2, t % 2 * 512
        gathered[n, :, lane : lane + 512] = jnp.dot(
            put_ref[...], part.astype(jnp.bfloat16), preferred_element_type=jnp.float32
        ).astype(jnp.bfloat16)
        if t % 2:
            outs.append(begin(gathered.at[n], out_ref.at[:, pl.ds(n * width, width)]))
    for copy in outs:
        copy.wait()


def run_experts(order, all_rows, take, put, weights_in, weights_down):
    far = pl.BlockSpec(memory_space=pltpu.HBM)
    local = pl.BlockSpec(memory_space=pltpu.VMEM)
    return pl.pallas_call(
        expert_kernel,
        out_shape=jax.ShapeDtypeStruct((ALL_ROWS, D), jnp.bfloat16),
        in_specs=[pl.BlockSpec(memory_space=pltpu.SMEM), far, local, local] + [far] * 15,
        out_specs=far,
        scratch_shapes=[
            pltpu.VMEM((CHUNKS, ALL_ROWS, D // CHUNKS), jnp.bfloat16),
            pltpu.VMEM((OWN_ROWS, D), jnp.bfloat16),
            pltpu.VMEM((N_TP, D, 256), jnp.bfloat16),
            pltpu.VMEM((N_TP, 1024, 512), jnp.bfloat16),
            pltpu.VMEM((N_TP, OWN_ROWS, 128), jnp.bfloat16),
            pltpu.VMEM((OWN_ROWS, 1024), jnp.bfloat16),
            pltpu.SemaphoreType.DMA((30,)),
        ],
        compiler_params=pltpu.CompilerParams(vmem_limit_bytes=46 << 20),
        name="experts",
    )(order, all_rows, take, put, *weights_in, weights_down)


def by_y(value, step):
    return lax.ppermute(value, "y", [(i, (i + step) % NY) for i in range(NY)])


def other_core(value):
    return lax.ppermute(value, "c", [(0, 1), (1, 0)])


def gather_pieces(own, below_top, above_bottom):
    half = own.shape[0] // 2
    far_top, far_bottom = by_y(below_top, 1), by_y(above_bottom, -1)
    below_bottom, above_top = by_y(own[half:], 1), by_y(own[:half], -1)
    pieces = [own, below_top, below_bottom, above_top, above_bottom, far_top, far_bottom]
    return pieces + [other_core(piece) for piece in pieces]


def three_parts(values):
    parts = []
    for _ in range(3):
        head = lax.reduce_precision(values, 8, 7)
        parts.append(head.astype(jnp.bfloat16))
        values = values - head
    return parts


def per_device(
    queries,
    fresh_kv,
    kv_pool,
    residual,
    norm_gain,
    gate_up,
    down_proj,
    prior_len,
    new_len,
    page_table,
    leaving,
    expert_ids,
    route_logits,
):
    my_z = lax.axis_index("z")
    my_group = lax.axis_index("x") * NZ + my_z
    leave_slot = leaving[my_group]
    handing = [(i, (i + 1) % N_REP) for i in range(N_REP)]

    in_own = gate_up[0]
    weights_down = lax.all_gather(down_proj[0], TP)
    mixed = jnp.concatenate(
        [queries.reshape(-1, N_TP, 512), fresh_kv.reshape(-1, N_TP, 256)], axis=2
    )
    heads = lax.all_to_all(mixed, TP, split_axis=1, concat_axis=0, tiled=True)[:, 0]
    heads, in_own = lax.optimization_barrier((heads, in_own))
    below_top, above_bottom = by_y(in_own[: D // 2], 1), by_y(in_own[D // 2 :], -1)
    query_heads, kv_rows = heads[:, :512], heads[:, 512:]
    resid_slots = residual.reshape(REQ, FRESH, -1)
    resid_came = lax.ppermute(
        lax.dynamic_index_in_dim(resid_slots, leave_slot, 0, keepdims=False), REP, handing
    )
    tables = page_table[0].reshape(REQ, PRIOR // PAGE)
    earlier = kv_pool[tables].reshape(REQ, PRIOR, -1)
    own_prior = lax.dynamic_slice_in_dim(prior_len, my_group * REQ, REQ, 0)
    own_new = lax.dynamic_slice_in_dim(new_len, my_group * REQ, REQ, 0)
    attention = attend_slots(
        query_heads.reshape(REQ, FRESH, -1),
        earlier,
        kv_rows.reshape(REQ, FRESH, -1),
        own_prior,
        own_new,
    )
    attention_came = lax.ppermute(
        lax.dynamic_index_in_dim(attention, leave_slot, 0, keepdims=False), REP, handing
    )
    is_new = (jnp.arange(REQ, dtype=jnp.int32) == leave_slot)[:, None, None]
    resid_new = jnp.where(is_new, resid_came[None], resid_slots).astype(jnp.float32)
    attention_new = jnp.where(is_new, attention_came[None], attention).astype(jnp.float32)
    token_count = REQ * FRESH
    hidden = (resid_new + attention_new).reshape(token_count, -1)

    struck = (
        expert_ids[:, :, None] == jnp.arange(EXPERTS, dtype=jnp.int32)[None, None, :]
    ).astype(jnp.bfloat16)
    loads = struck[:, 0] + struck[:, 1]
    earlier_rows = (
        jnp.arange(token_count, dtype=jnp.int32)[:, None]
        > jnp.arange(token_count, dtype=jnp.int32)[None, :]
    ).astype(jnp.bfloat16)
    ahead = jnp.dot(earlier_rows, loads, preferred_element_type=jnp.float32)
    place = jnp.sum(struck.astype(jnp.float32) * ahead[:, None, :], axis=2).astype(jnp.int32)
    target = (
        ((expert_ids // 2) * N_TP + place // SHARE) * PIECE + (expert_ids % 2) * SHARE + place % SHARE
    )
    slots = jnp.arange(EXPERTS * CAP, dtype=jnp.int32)
    placing = (
        (target[:, 0][None, :] == slots[:, None]) | (target[:, 1][None, :] == slots[:, None])
    ).astype(jnp.bfloat16)

    squares = three_parts(jnp.sum(hidden * hidden, axis=1))
    extra = jnp.stack(squares + [jnp.zeros_like(squares[0])], axis=1)
    extra = jnp.pad(extra, ((0, 0), (0, WIDE - 512 - 4)))
    payload = jnp.concatenate(
        [(hidden * norm_gain[None, :]).astype(jnp.bfloat16), extra], axis=1
    )
    packed = jnp.dot(placing, payload, preferred_element_type=jnp.float32).astype(jnp.bfloat16)
    received = lax.all_to_all(packed.reshape(NX * N_TP, PIECE, WIDE), SPREAD, 0, 0)
    normed = norm_rows(received.reshape(NX * N_TP, PIECE, WIDE))
    normed, in_own, weights_down, below_top, above_bottom = lax.optimization_barrier(
        (normed, in_own, weights_down, below_top, above_bottom)
    )
    all_rows = lax.all_gather(normed, "z", tiled=True)
    weights_in = gather_pieces(in_own, below_top, above_bottom)
    my_y, my_core = lax.axis_index("y"), lax.axis_index("c")
    piece = jnp.arange(N_TP, dtype=jnp.int32)
    step = piece % 4
    step = jnp.where(step == 1, NY - 1, jnp.where(step == 2, 1, jnp.where(step == 3, 2, 0)))
    order = (my_y + step) % NY * NC + (my_core + piece // 4) % NC

    index = jnp.arange(ALL_ROWS, dtype=jnp.int32)
    own = (index // SHARE) % 2 == my_z // 8
    compact = jnp.where(own, (index // PIECE) * SHARE + index % SHARE, -1)
    own_index = jnp.arange(OWN_ROWS, dtype=jnp.int32)
    take = (own_index[:, None] == compact[None, :]).astype(jnp.bfloat16)
    put = (compact[:, None] == own_index[None, :]).astype(jnp.bfloat16)
    partial_rows = run_experts(order, all_rows, take, put, weights_in, weights_down)
    summed = lax.psum_scatter(partial_rows, "z", scatter_dimension=0, tiled=True)
    back = summed.reshape(NX, PIECE, N_TP, 512).transpose(0, 2, 1, 3)
    returned = lax.all_to_all(back.reshape(NX * N_TP, PIECE, 512), SPREAD, 0, 0)
    returned = returned.reshape(EXPERTS * CAP, 512)
    shares = jax.nn.softmax(route_logits, axis=-1)
    first = (target[:, 0][:, None] == slots[None, :]).astype(jnp.bfloat16)
    second = (target[:, 1][:, None] == slots[None, :]).astype(jnp.bfloat16)
    moe_out = shares[:, 0:1] * jnp.dot(
        first, returned, preferred_element_type=jnp.float32
    ) + shares[:, 1:2] * jnp.dot(second, returned, preferred_element_type=jnp.float32)
    return (hidden + moe_out).astype(jnp.bfloat16)


def solution(mesh):
    inner = Mesh(mesh.devices.reshape(NX, NZ, NY, NC), ("x", "z", "y", "c"))
    every = ("x", "z", "y", "c")
    in_specs = (
        P(every, None),
        P(every, None),
        P(REP, None, TP),
        P(REP, TP),
        P(TP),
        P(REP, None, TP),
        P(REP, None, TP),
        P(),
        P(),
        P(REP, None),
        P(),
        P(REP, None),
        P(REP, None),
    )
    return jax.shard_map(
        per_device, mesh=inner, in_specs=in_specs, out_specs=P(REP, TP), check_vma=False
    )
```
